32 devices in a mesh: section: 4 (over y, core), tensor: 8 (over z, x).
Axes of the slice: x: 2, y: 2, z: 4, core: 2. Of those that a mesh axis runs over, the one named last changes fastest.
Arguments:
- carry_in: bfloat16 [4, 2, 16, 4096], P('section', None, 'tensor'), may hold values from -6 to 6
- norm_gain: float32 [4, 4096], P('section'), may hold values from 0.5 to 1.5
- w_gate: bfloat16 [4, 384, 128, 128], P('section', 'tensor'), may hold values from -0.15625 to 0.15625
- w_up: bfloat16 [4, 384, 128, 128], P('section', 'tensor'), may hold values from -0.15625 to 0.15625
- w_down: bfloat16 [4, 384, 128, 128], P('section', 'tensor'), may hold values from -0.15625 to 0.15625
- tile_list: int32 [4, 384], P('section', 'tensor'), may hold values from 0 to 128, as said below
- grad_in: bfloat16 [4, 2, 16, 4096], P('section', None, 'tensor'), may hold values from -6 to 6
Outputs:
- section_out: bfloat16 [4, 2, 16, 4096], P('section', None, 'tensor')
- grad_back: bfloat16 [4, 2, 16, 4096], P('section', None, 'tensor')
The draws below stay inside these ranges and needn't reach their ends.
Inputs may be any that keep to these rules, and one draw needn't show every extreme that they name: `tile_list`: for each layer and tensor index t, entries 48 * t to 48 * t + 47 list distinct tile numbers f * 32 + c (f a block of that device's hidden units, c a block of features) in rising order, followed by the padding value 4 * 32. Each such list has at least 24 live entries, and in every layer some tensor index has all 48 live.
All inputs are finite; a program needn't handle non-finite values.
Results may differ from the reference program's by a relative error of at most 0.013.
Values may be sent and summed in bfloat16 or wider, within the bound.
A program may use at most 64 MiB of HBM per device.

```python
import jax
import jax.numpy as jnp
from jax import lax

D = 4096
BLK = 128
FB_DEV = 4
SLOTS = 48
MB = 2
TOK = 16
N_SECTION = 4
N_TENSOR = 8


def draw_tile_list(key, part):
    key_order = jax.random.fold_in(key, 11)
    key_count = jax.random.fold_in(key, 23)
    key_busy = jax.random.fold_in(key, 37)
    grid = FB_DEV * (D // BLK)
    scores = jax.random.randint(key_order, (N_SECTION, N_TENSOR, grid), 0, 1 << 20)
    cells = jnp.arange(grid, dtype=jnp.int32)
    ranked = jnp.argsort(scores * grid + cells[None, None, :], axis=-1)[:, :, :SLOTS]
    ranked = jnp.sort(ranked.astype(jnp.int32), axis=-1)
    counts = jax.random.randint(key_count, (N_SECTION, N_TENSOR), SLOTS // 2, SLOTS + 1)
    busiest = jax.random.randint(key_busy, (N_SECTION,), 0, N_TENSOR)
    devices = jnp.arange(N_TENSOR, dtype=jnp.int32)
    counts = jnp.where(devices[None, :] == busiest[:, None], SLOTS, counts)
    slots = jnp.arange(SLOTS, dtype=jnp.int32)
    listed = jnp.where(slots[None, None, :] < counts[:, :, None], ranked, grid)
    return listed.reshape(N_SECTION, N_TENSOR * SLOTS).astype(jnp.int32)


def shard_levels(own_key, dims, cuts, low, high):
    def one(position, blocks):
        draws = jax.random.uniform(jax.random.fold_in(jax.random.fold_in(own_key, 6), position), (blocks,), jnp.float32, low / len(cuts), high / len(cuts))
        return jnp.repeat(jnp.exp(draws), dims[position] // blocks).reshape((-1,) + (1,) * (len(dims) - position - 1))

    loudness = one(*cuts[0])
    for cut in cuts[1:]:
        loudness = loudness * one(*cut)
    return loudness


def bell_draw(rng, extent, deviation, reach, split=(), kind=jnp.bfloat16):
    level = shard_levels(rng, extent, split, -0.22, 0.18) if split else 1.0
    array = jax.random.normal(rng, extent, jnp.float32) * deviation * level
    return jnp.minimum(jnp.maximum(array, -reach), reach).astype(kind)


def setup_inputs(seed: int = 0) -> dict:
    splits = jax.random.split(jax.random.key(seed), 8)
    return {
        "carry_in": bell_draw(splits[0], (N_SECTION, MB, TOK, D), 1.0, 6.0, ((0, 4), (2, 8))),
        "norm_gain": jnp.clip(1.0 + 0.1 * jax.random.normal(splits[1], (N_SECTION, D), jnp.float32), 0.5, 1.5),
        "w_gate": bell_draw(splits[2], (N_SECTION, N_TENSOR * SLOTS, BLK, BLK), (BLK * SLOTS // FB_DEV) ** -0.5, 0.15625, ((0, 4), (1, 8))),
        "w_up": bell_draw(splits[3], (N_SECTION, N_TENSOR * SLOTS, BLK, BLK), (BLK * SLOTS // FB_DEV) ** -0.5, 0.15625, ((0, 4), (1, 8))),
        "w_down": bell_draw(splits[4], (N_SECTION, N_TENSOR * SLOTS, BLK, BLK), (max(BLK, BLK * N_TENSOR * SLOTS // (D // BLK))) ** -0.5, 0.15625, ((0, 4), (1, 8))),
        "tile_list": draw_tile_list(jax.random.fold_in(splits[7], 71), 0),
        "grad_in": bell_draw(splits[6], (N_SECTION, MB, TOK, D), 1.0, 6.0, ((0, 4), (2, 8))),
    }


EPS = 1e-05
HIGH = lax.Precision.HIGHEST

def tile_tables(tile_ids, fblocks, dblocks):
    live = tile_ids < fblocks * dblocks
    safe = jnp.where(live, tile_ids, 0).astype(jnp.int32)
    f_of = safe // dblocks
    d_of = safe - f_of * dblocks
    pick_f = jnp.logical_and(f_of[:, None] == jnp.arange(fblocks, dtype=jnp.int32)[None, :], live[:, None])
    pick_d = jnp.logical_and(d_of[:, None] == jnp.arange(dblocks, dtype=jnp.int32)[None, :], live[:, None])
    return (pick_f.astype(jnp.float32), pick_d.astype(jnp.float32))

def rms_scale(values):
    return lax.rsqrt(lax.optimization_barrier(jnp.mean(values * values, axis=-1, keepdims=True)) + EPS)

def ein(form, left, right):
    return jnp.einsum(form, left.astype(jnp.float32), right.astype(jnp.float32), precision=HIGH)

def one_section(section_args):
    x_in, gain, gate_tiles, up_tiles, down_tiles, tile_ids, grad_out = section_args
    dblocks = D // BLK
    rows = x_in.reshape(MB * TOK, D)
    scale = rms_scale(rows)
    normed = (rows * scale * gain).astype(jnp.bfloat16).reshape(MB * TOK, dblocks, BLK)
    grad_rows = grad_out.reshape(MB * TOK, dblocks, BLK)
    gate_tiles = gate_tiles.reshape(N_TENSOR, SLOTS, BLK, BLK)
    up_tiles = up_tiles.reshape(N_TENSOR, SLOTS, BLK, BLK)
    down_tiles = down_tiles.reshape(N_TENSOR, SLOTS, BLK, BLK)
    tile_ids = tile_ids.reshape(N_TENSOR, SLOTS)

    def one_device(carry, device_args):
        ffn_total, back_total = carry
        gate_w, up_w, down_w, ids_here = device_args
        pick_f, pick_d = tile_tables(ids_here, FB_DEV, dblocks)
        chosen = ein('rdc,kd->rkc', normed, pick_d)
        gate = ein('rke,kf->rfe', ein('rkc,kce->rke', chosen, gate_w), pick_f)
        up_proj = ein('rke,kf->rfe', ein('rkc,kce->rke', chosen, up_w), pick_f)
        hidden = (jax.nn.silu(gate) * up_proj).astype(jnp.bfloat16)
        spread = ein('rfc,kf->rkc', hidden, pick_f)
        term = ein('rke,kd->rde', ein('rkc,kce->rke', spread, down_w), pick_d)
        term = lax.optimization_barrier(term.astype(jnp.bfloat16)).astype(jnp.float32)
        picked = ein('rde,kd->rke', grad_rows, pick_d)
        d_hidden = ein('rkc,kf->rfc', ein('rke,kce->rkc', picked, down_w), pick_f)
        sigmoid_gate = jax.nn.sigmoid(gate)
        d_gate = (d_hidden * up_proj * sigmoid_gate * (1.0 + gate * (1.0 - sigmoid_gate))).astype(jnp.bfloat16)
        d_up = (d_hidden * gate * sigmoid_gate).astype(jnp.bfloat16)
        gate_spread = ein('rfe,kf->rke', d_gate, pick_f)
        up_spread = ein('rfe,kf->rke', d_up, pick_f)
        inner = ein('rke,kce->rkc', gate_spread, gate_w) + ein('rke,kce->rkc', up_spread, up_w)
        back = ein('rkc,kd->rdc', inner, pick_d)
        back = lax.optimization_barrier(back.astype(jnp.bfloat16)).astype(jnp.float32)
        return ((ffn_total + term, back_total + back), None)
    empty = jnp.zeros((MB * TOK, dblocks, BLK), jnp.float32)
    (ffn_total, back_total), _ = lax.scan(one_device, (empty, empty), (gate_tiles, up_tiles, down_tiles, tile_ids))
    ffn_total = ffn_total.reshape(MB * TOK, D)
    grad_normed = back_total.reshape(MB * TOK, D)
    output = (rows + ffn_total).astype(jnp.bfloat16)
    mixed = lax.optimization_barrier(jnp.mean(rows * gain * grad_normed, axis=-1, keepdims=True))
    grad_x = grad_out.reshape(MB * TOK, D).astype(jnp.float32) + scale * gain * grad_normed - rows * scale ** 3 * mixed
    return (output.reshape(MB, TOK, D), grad_x.astype(jnp.bfloat16).reshape(MB, TOK, D))

def reference(carry_in, norm_gain, w_gate, w_up, w_down, tile_list, grad_in):
    x_all = jnp.roll(carry_in, 1, axis=0).astype(jnp.float32)
    outputs, grads = lax.map(one_section, (x_all, norm_gain.astype(jnp.float32), w_gate, w_up, w_down, tile_list, grad_in))
    return (outputs, jnp.roll(grads, -1, axis=0))
```

```python
import functools

import jax
import jax.numpy as jnp
from jax import lax
from jax.experimental import pallas as pl
from jax.experimental.pallas import tpu as pltpu
from jax.sharding import PartitionSpec as P

FB_DEV = 4
EPS = 1e-05
PAIR = 2
MESH = pl.DeviceIdType.MESH
NT = (((1,), (1,)), ((), ()))


def kernel(
    sections, tensors,
    tl_h, carry, gain, wg_h, wu_h, wd_h, dy_h,
    out, gback,
    xg, dyg, dyn, gn, gv, cown, wg, wu, wd, nb, db, xs, gu, dh, part, hb, dgu,
    stage, xr, zs, zr, tl, inv, last, lsem, ssem, rsem,
):
    line = tensors // PAIR
    mb, tokd, width = carry.shape[1:]
    per = mb * tokd
    half = line * per
    rows = PAIR * half
    blk = wg.shape[-1]
    slots = wg.shape[0]
    dblocks = width // blk
    s = lax.axis_index("section")
    t = lax.axis_index("tensor")
    z, x = t // PAIR, t % PAIR
    s_next, s_prev = (s + 1) % sections, (s + sections - 1) % sections

    def dev(sec, zt, other=False):
        return (sec, zt * PAIR + ((PAIR - 1 - x) if other else x))

    local = [
        pltpu.make_async_copy(tl_h, tl, lsem.at[6]),
        pltpu.make_async_copy(carry.at[0], cown, lsem.at[5]),
        pltpu.make_async_copy(dy_h.at[0], dyg.at[0, z], lsem.at[0]),
        pltpu.make_async_copy(gain, gv, lsem.at[4]),
        pltpu.make_async_copy(wg_h.at[0], wg, lsem.at[2]),
        pltpu.make_async_copy(wu_h.at[0], wu, lsem.at[3]),
        pltpu.make_async_copy(wd_h.at[0], wd, lsem.at[1]),
    ]
    for c in local:
        c.start()

    offsets = sorted((o for o in range(1 - line, line) if o), key=abs)

    def each(offs, body):
        for o in offs:
            zt = z + o

            @pl.when(jnp.logical_and(zt >= 0, zt < line))
            def _(zt=zt):
                body(zt)

    barrier = pltpu.get_barrier_semaphore()

    def greet(to):
        pl.semaphore_signal(barrier, inc=1, device_id=to, device_id_type=MESH)

    each(offsets, lambda zt: greet(dev(s, zt)))
    for zt in range(line):
        greet(dev(s_next, zt))
        greet(dev(s_prev, zt))
    for sec in (s, s_next, s_prev):
        greet(dev(sec, z, True))
    pl.semaphore_wait(barrier, (line - 1) + 2 * line + 3)

    def remote(src, dst, si, ri, to):
        return pltpu.make_async_remote_copy(
            src_ref=src, dst_ref=dst, send_sem=ssem.at[si], recv_sem=rsem.at[ri],
            device_id=to, device_id_type=MESH,
        )

    XZ, XX, DYZ, DYX, FX, BX, FZ, BZ = (i * line for i in range(8))
    DYB, GNB = 8 * line, 8 * line + 1
    mate = dev(s, z, True)

    def x_line(zt):
        return remote(carry.at[0], xg.at[0, z], XZ + zt, XZ + z, dev(s_next, zt))

    def x_mate():
        return remote(carry.at[0], xg.at[1, z], XX + z, XX + z, dev(s_next, z, True))

    def x_relay(zt):
        return remote(xg.at[0, zt], xg.at[1, zt], XX + zt, XX + zt, mate)

    def dy_line(zt):
        return remote(dy_h.at[0], dyg.at[0, z], DYZ + zt, DYZ + z, dev(s, zt))

    def dy_mate():
        return remote(dy_h.at[0], dyg.at[1, z], DYX + z, DYX + z, mate)

    def dy_relay(zt):
        return remote(dyg.at[0, zt], dyg.at[1, zt], DYX + zt, DYX + zt, mate)

    def dy_back():
        return remote(dy_h.at[0], dyn, DYB, DYB, dev(s_prev, z))

    def gain_back():
        return remote(gain, gn, GNB, GNB, dev(s_prev, z))

    def got(dst, ri):
        remote(dst, dst, ri, ri, mate).wait_recv()

    each(offsets, lambda zt: x_line(zt).start())
    x_line(z).start()
    x_mate().start()
    dy_mate().start()
    each(offsets, lambda zt: dy_line(zt).start())
    dy_back().start()
    gain_back().start()

    local[0].wait()
    p = jnp.int32(0)
    for f in range(FB_DEV):
        def cell(i, p, f=f):
            q = f * dblocks + i
            hit = tl[0, jnp.minimum(p, slots - 1)] == q
            inv[q] = jnp.where(hit, p, slots)
            return p + hit.astype(jnp.int32)
        p_new = lax.fori_loop(0, dblocks, cell, p, unroll=4)
        last[f] = jnp.where(p_new > p, p_new - 1, slots)
        p = p_new
    gu[slots] = jnp.zeros((rows, 2 * blk), jnp.float32)
    dh[slots] = jnp.zeros((rows, blk), jnp.float32)
    part[slots] = jnp.zeros((rows, blk), jnp.float32)

    def rows_of(ref, c, h):
        cols = pl.ds(pl.multiple_of(c * blk, blk), blk)
        pieces = []
        for d in range(line):
            for m in range(mb):
                pieces.append(ref[h, d, m, :, cols].astype(jnp.float32))
        return jnp.concatenate(pieces, axis=0)

    def f_of(k):
        return jnp.minimum(tl[0, k] // dblocks, FB_DEV - 1)

    def c_of(k):
        return tl[0, k] % dblocks

    def keep_of(k):
        return (f_of(k) == f_of(jnp.maximum(k - 1, 0))).astype(jnp.float32)

    def square(h):
        def body(c, acc):
            v = rows_of(xg, c, h)
            xs[c, h * half:(h + 1) * half] = v
            return acc + v * v
        return lax.fori_loop(0, dblocks, body, jnp.zeros((half, blk), jnp.float32), unroll=4)

    def pack_dy(h):
        @pl.loop(0, dblocks, unroll=4)
        def _(c):
            db[c, h * half:(h + 1) * half] = rows_of(dyg, c, h).astype(jnp.bfloat16)

    def relay_x(zt):
        got(xg.at[0, zt], XZ + zt)
        x_relay(zt).start()
    each(offsets, relay_x)
    got(xg.at[0, z], XZ + z)
    acc_own = square(0)
    def relay_dy(zt):
        got(dyg.at[0, zt], DYZ + zt)
        dy_relay(zt).start()
    each(offsets, relay_dy)
    for c in local[1:]:
        c.wait()
    pack_dy(0)
    for zt in range(line):
        got(xg.at[1, zt], XX + zt)
    acc = jnp.concatenate([acc_own, square(1)], axis=0)
    scale = lax.rsqrt(jnp.sum(acc, axis=-1, keepdims=True) / width + EPS)

    @pl.loop(0, dblocks, unroll=4)
    def _(c):
        cols = pl.ds(pl.multiple_of(c * blk, blk), blk)
        nb[c] = (xs[c] * scale * gv[:, cols]).astype(jnp.bfloat16)

    def g_step(k, cur):
        w = jnp.concatenate([wg[k], wu[k]], axis=1)
        new = jnp.dot(nb[c_of(k)], w, preferred_element_type=jnp.float32)
        cur = cur * keep_of(k) + new
        gu[k] = cur
        return cur
    lax.fori_loop(0, slots, g_step, jnp.zeros((rows, 2 * blk), jnp.float32), unroll=16)

    for f in range(FB_DEV):
        both = gu[last[f]]
        g, u = both[:, :blk], both[:, blk:]
        hb[f] = (g * jax.nn.sigmoid(g) * u).astype(jnp.bfloat16)

    def collect(a):
        @pl.loop(0, dblocks, unroll=4)
        def _(c):
            cols = pl.ds(pl.multiple_of(c * blk, blk), blk)
            total = part[inv[c]]
            for f in range(1, FB_DEV):
                total = total + part[inv[f * dblocks + c]]
            for h in range(PAIR):
                for d in range(line):
                    r = (h * line + d) * per
                    stage[a, h, d, :, cols] = total[r:r + per].astype(jnp.bfloat16)

    chunks = sorted(range(line), key=lambda d: min(2 * d, 2 * (line - 1 - d) + 1))

    def swap(a, base, zt):
        return remote(stage.at[a, 1, zt], xr.at[a, zt], base + zt, base + zt, mate)

    def f_out(zt):
        return remote(zs.at[0, zt], zr.at[0, z], FZ + zt, FZ + z, dev(s, zt))

    def b_out(zt):
        return remote(zs.at[1, zt], zr.at[1, z], BZ + zt, BZ + z, dev(s_prev, zt))

    def o_step(k, _):
        part[k] = jnp.dot(hb[f_of(k)], wd[k], preferred_element_type=jnp.float32)
        return 0
    lax.fori_loop(0, slots, o_step, 0, unroll=16)
    collect(0)
    for zt in chunks:
        swap(0, FX, zt).start()

    for zt in range(line):
        got(dyg.at[1, zt], DYX + zt)
    pack_dy(1)

    def d_step(k, cur):
        new = lax.dot_general(db[c_of(k)], wd[k], NT, preferred_element_type=jnp.float32)
        cur = cur * keep_of(k) + new
        dh[k] = cur
        return cur
    lax.fori_loop(0, slots, d_step, jnp.zeros((rows, blk), jnp.float32), unroll=16)

    for f in range(FB_DEV):
        both = gu[last[f]]
        g, u = both[:, :blk], both[:, blk:]
        sg = jax.nn.sigmoid(g)
        dv = dh[last[f]]
        dgu[f, :, :blk] = (dv * u * sg * (1.0 + g * (1.0 - sg))).astype(jnp.bfloat16)
        dgu[f, :, blk:] = (dv * g * sg).astype(jnp.bfloat16)

    def b_step(k, _):
        w = jnp.concatenate([wg[k], wu[k]], axis=1)
        part[k] = lax.dot_general(dgu[f_of(k)], w, NT, preferred_element_type=jnp.float32)
        return 0
    lax.fori_loop(0, slots, b_step, 0, unroll=16)
    collect(1)
    for zt in chunks:
        swap(1, BX, zt).start()

    def pair_sum(a, zt):
        return stage[a, 0, zt].astype(jnp.float32) + xr[a, zt].astype(jnp.float32)

    for zt in chunks:
        got(xr.at[0, zt], FX + zt)
        zs[0, zt] = pair_sum(0, zt).astype(jnp.bfloat16)

        @pl.when(z != zt)
        def _(zt=zt):
            f_out(zt).start()
    for zt in chunks:
        got(xr.at[1, zt], BX + zt)
        zs[1, zt] = pair_sum(1, zt).astype(jnp.bfloat16)
        b_out(zt).start()

    zr[0, z] = zs[0, z]
    each(offsets, lambda zt: got(zr.at[0, zt], FZ + zt))
    ffn = zr[0, 0].astype(jnp.float32)
    for d in range(1, line):
        ffn = ffn + zr[0, d].astype(jnp.float32)
    for m in range(mb):
        xo = xg[0, z, m].astype(jnp.float32)
        out[0, m] = (xo + ffn[m * tokd:(m + 1) * tokd]).astype(jnp.bfloat16)

    each(offsets, lambda zt: x_line(zt).wait_send())
    x_line(z).wait_send()
    x_mate().wait_send()
    each(offsets, lambda zt: x_relay(zt).wait_send())
    dy_mate().wait_send()
    each(offsets, lambda zt: dy_line(zt).wait_send())
    each(offsets, lambda zt: dy_relay(zt).wait_send())
    dy_back().wait_send()
    gain_back().wait_send()
    for zt in range(line):
        swap(0, FX, zt).wait_send()
        swap(1, BX, zt).wait_send()
    each(offsets, lambda zt: f_out(zt).wait_send())
    got(dyn, DYB)
    got(gn, GNB)
    for zt in range(line):
        got(zr.at[1, zt], BZ + zt)
    gnorm = zr[1, 0].astype(jnp.float32)
    for d in range(1, line):
        gnorm = gnorm + zr[1, d].astype(jnp.float32)
    for m in range(mb):
        xo = cown[m].astype(jnp.float32)
        sc = lax.rsqrt(jnp.mean(xo * xo, axis=-1, keepdims=True) + EPS)
        gg = gn[...] * gnorm[m * tokd:(m + 1) * tokd]
        mixed = jnp.mean(xo * gg, axis=-1, keepdims=True)
        gx = dyn[m].astype(jnp.float32) + sc * gg - xo * (sc * sc * sc) * mixed
        gback[0, m] = gx.astype(jnp.bfloat16)
    for zt in range(line):
        b_out(zt).wait_send()


def on_device(sections, tensors, carry_in, norm_gain, w_gate, w_up, w_down, tile_list, grad_in):
    _, mb, tokd, width = carry_in.shape
    slots, blk = w_gate.shape[1], w_gate.shape[-1]
    line = tensors // PAIR
    per = mb * tokd
    half = line * per
    rows = PAIR * half
    dblocks = width // blk
    bf, f32 = jnp.bfloat16, jnp.float32
    V = pltpu.VMEM
    anyspec = pl.BlockSpec(memory_space=pl.ANY)
    nsem = 8 * line + 2
    parts = pl.pallas_call(
        functools.partial(kernel, sections, tensors),
        out_shape=[jax.ShapeDtypeStruct(carry_in.shape, bf)] * 2,
        in_specs=[anyspec] * 7,
        out_specs=[pl.BlockSpec(memory_space=pltpu.VMEM)] * 2,
        scratch_shapes=[
            V((PAIR, line, mb, tokd, width), bf),
            V((PAIR, line, mb, tokd, width), bf),
            V((mb, tokd, width), bf),
            V((1, width), f32),
            V((1, width), f32),
            V((mb, tokd, width), bf),
            V((slots, blk, blk), bf),
            V((slots, blk, blk), bf),
            V((slots, blk, blk), bf),
            V((dblocks, rows, blk), bf),
            V((dblocks, rows, blk), bf),
            V((dblocks, rows, blk), f32),
            V((slots + 1, rows, 2 * blk), f32),
            V((slots + 1, rows, blk), f32),
            V((slots + 1, rows, blk), f32),
            V((FB_DEV, rows, blk), bf),
            V((FB_DEV, rows, 2 * blk), bf),
            V((2, PAIR, line, per, width), bf),
            V((2, line, per, width), bf),
            V((2, line, per, width), bf),
            V((2, line, per, width), bf),
            pltpu.SMEM((1, slots), jnp.int32),
            pltpu.SMEM((FB_DEV * dblocks,), jnp.int32),
            pltpu.SMEM((FB_DEV,), jnp.int32),
            pltpu.SemaphoreType.DMA((7,)),
            pltpu.SemaphoreType.DMA((nsem,)),
            pltpu.SemaphoreType.DMA((nsem,)),
        ],
        compiler_params=pltpu.CompilerParams(
            collective_id=0, has_side_effects=True, vmem_limit_bytes=56 * 1024 * 1024
        ),
    )(tile_list, carry_in, norm_gain, w_gate, w_up, w_down, grad_in)
    return pl.pallas_call(
        store,
        out_shape=[jax.ShapeDtypeStruct(carry_in.shape, bf)] * 2,
        in_specs=[pl.BlockSpec(memory_space=pltpu.VMEM)] * 2,
        out_specs=[anyspec] * 2,
        scratch_shapes=[pltpu.SemaphoreType.DMA((2,))],
    )(*parts)


def store(a, b, out_a, out_b, sem):
    copies = [
        pltpu.make_async_copy(a, out_a, sem.at[0]),
        pltpu.make_async_copy(b, out_b, sem.at[1]),
    ]
    for c in copies:
        c.start()
    for c in copies:
        c.wait()


def solution(mesh):
    placed = (
        P("section", None, "tensor", None),
        P("section", None),
        P("section", "tensor", None, None),
        P("section", "tensor", None, None),
        P("section", "tensor", None, None),
        P("section", "tensor"),
        P("section", None, "tensor", None),
    )
    return jax.shard_map(
        functools.partial(on_device, mesh.shape["section"], mesh.shape["tensor"]),
        mesh=mesh,
        in_specs=placed,
        out_specs=(P("section", None, "tensor", None), P("section", None, "tensor", None)),
        check_vma=False,
    )
```

```python
import functools

import jax
import jax.numpy as jnp
from jax import lax
from jax.experimental import pallas as pl
from jax.experimental.pallas import tpu as pltpu
from jax.sharding import PartitionSpec as P

FB_DEV = 4
EPS = 1e-05
PAIR = 2
MESH = pl.DeviceIdType.MESH
NT = (((1,), (1,)), ((), ()))


def kernel(
    sections, tensors,
    tl_h, carry, gain, wg_h, wu_h, wd_h, dy_h,
    out, gback,
    xg, dyg, dyn, gn, gv, cown, wg, wu, wd, nb, db, xs, gu, dh, part, hb, dgu,
    stage, xr, zs, zr, tl, inv, last, lsem, ssem, rsem,
):
    line = tensors // PAIR
    mb, tokd, width = carry.shape[1:]
    per = mb * tokd
    half = line * per
    rows = PAIR * half
    blk = wg.shape[-1]
    slots = wg.shape[0]
    dblocks = width // blk
    s = lax.axis_index("section")
    t = lax.axis_index("tensor")
    z, x = t // PAIR, t % PAIR
    s_next, s_prev = (s + 1) % sections, (s + sections - 1) % sections

    def dev(sec, zt, other=False):
        return (sec, zt * PAIR + ((PAIR - 1 - x) if other else x))

    local = [
        pltpu.make_async_copy(tl_h, tl, lsem.at[6]),
        pltpu.make_async_copy(carry.at[0], cown, lsem.at[5]),
        pltpu.make_async_copy(dy_h.at[0], dyg.at[0, z], lsem.at[0]),
        pltpu.make_async_copy(gain, gv, lsem.at[4]),
        pltpu.make_async_copy(wg_h.at[0], wg, lsem.at[2]),
        pltpu.make_async_copy(wu_h.at[0], wu, lsem.at[3]),
        pltpu.make_async_copy(wd_h.at[0], wd, lsem.at[1]),
    ]
    for c in local:
        c.start()

    offsets = sorted((o for o in range(1 - line, line) if o), key=abs)

    def each(offs, body):
        for o in offs:
            zt = z + o

            @pl.when(jnp.logical_and(zt >= 0, zt < line))
            def _(zt=zt):
                body(zt)

    barrier = pltpu.get_barrier_semaphore()

    def greet(to):
        pl.semaphore_signal(barrier, inc=1, device_id=to, device_id_type=MESH)

    each(offsets, lambda zt: greet(dev(s, zt)))
    for zt in range(line):
        greet(dev(s_next, zt))
        greet(dev(s_prev, zt))
    for sec in (s, s_next, s_prev):
        greet(dev(sec, z, True))
    pl.semaphore_wait(barrier, (line - 1) + 2 * line + 3)

    def remote(src, dst, si, ri, to):
        return pltpu.make_async_remote_copy(
            src_ref=src, dst_ref=dst, send_sem=ssem.at[si], recv_sem=rsem.at[ri],
            device_id=to, device_id_type=MESH,
        )

    XZ, XX, DYZ, DYX, FX, BX, FZ, BZ = (i * line for i in range(8))
    DYB, GNB = 8 * line, 8 * line + 1
    mate = dev(s, z, True)

    def x_line(zt):
        return remote(carry.at[0], xg.at[0, z], XZ + zt, XZ + z, dev(s_next, zt))

    def x_mate():
        return remote(carry.at[0], xg.at[1, z], XX + z, XX + z, dev(s_next, z, True))

    def x_relay(zt):
        return remote(xg.at[0, zt], xg.at[1, zt], XX + zt, XX + zt, mate)

    def dy_line(zt):
        return remote(dy_h.at[0], dyg.at[0, z], DYZ + zt, DYZ + z, dev(s, zt))

    def dy_mate():
        return remote(dy_h.at[0], dyg.at[1, z], DYX + z, DYX + z, mate)

    def dy_relay(zt):
        return remote(dyg.at[0, zt], dyg.at[1, zt], DYX + zt, DYX + zt, mate)

    def dy_back():
        return remote(dy_h.at[0], dyn, DYB, DYB, dev(s_prev, z))

    def gain_back():
        return remote(gain, gn, GNB, GNB, dev(s_prev, z))

    def got(dst, ri):
        remote(dst, dst, ri, ri, mate).wait_recv()

    each(offsets, lambda zt: x_line(zt).start())
    x_line(z).start()
    x_mate().start()
    dy_mate().start()
    each(offsets, lambda zt: dy_line(zt).start())
    dy_back().start()
    gain_back().start()

    local[0].wait()
    p = jnp.int32(0)
    for f in range(FB_DEV):
        def cell(i, p, f=f):
            q = f * dblocks + i
            hit = tl[0, jnp.minimum(p, slots - 1)] == q
            inv[q] = jnp.where(hit, p, slots)
            return p + hit.astype(jnp.int32)
        p_new = lax.fori_loop(0, dblocks, cell, p, unroll=4)
        last[f] = jnp.where(p_new > p, p_new - 1, slots)
        p = p_new
    gu[slots] = jnp.zeros((rows, 2 * blk), jnp.float32)
    dh[slots] = jnp.zeros((rows, blk), jnp.float32)
    part[slots] = jnp.zeros((rows, blk), jnp.float32)

    def rows_of(ref, c, h):
        cols = pl.ds(pl.multiple_of(c * blk, blk), blk)
        pieces = []
        for d in range(line):
            for m in range(mb):
                pieces.append(ref[h, d, m, :, cols].astype(jnp.float32))
        return jnp.concatenate(pieces, axis=0)

    def f_of(k):
        return jnp.minimum(tl[0, k] // dblocks, FB_DEV - 1)

    def c_of(k):
        return tl[0, k] % dblocks

    def keep_of(k):
        return (f_of(k) == f_of(jnp.maximum(k - 1, 0))).astype(jnp.float32)

    def square(h):
        def body(c, acc):
            v = rows_of(xg, c, h)
            xs[c, h * half:(h + 1) * half] = v
            return acc + v * v
        return lax.fori_loop(0, dblocks, body, jnp.zeros((half, blk), jnp.float32), unroll=4)

    def pack_dy(h):
        @pl.loop(0, dblocks, unroll=4)
        def _(c):
            db[c, h * half:(h + 1) * half] = rows_of(dyg, c, h).astype(jnp.bfloat16)

    def relay_x(zt):
        got(xg.at[0, zt], XZ + zt)
        x_relay(zt).start()
    each(offsets, relay_x)
    got(xg.at[0, z], XZ + z)
    acc_own = square(0)
    def relay_dy(zt):
        got(dyg.at[0, zt], DYZ + zt)
        dy_relay(zt).start()
    each(offsets, relay_dy)
    for c in local[1:]:
        c.wait()
    pack_dy(0)
    for zt in range(line):
        got(xg.at[1, zt], XX + zt)
    acc = jnp.concatenate([acc_own, square(1)], axis=0)
    scale = lax.rsqrt(jnp.sum(acc, axis=-1, keepdims=True) / width + EPS)

    @pl.loop(0, dblocks, unroll=4)
    def _(c):
        cols = pl.ds(pl.multiple_of(c * blk, blk), blk)
        nb[c] = (xs[c] * scale * gv[:, cols]).astype(jnp.bfloat16)

    def g_step(k, cur):
        w = jnp.concatenate([wg[k], wu[k]], axis=1)
        new = jnp.dot(nb[c_of(k)], w, preferred_element_type=jnp.float32)
        cur = cur * keep_of(k) + new
        gu[k] = cur
        return cur
    lax.fori_loop(0, slots, g_step, jnp.zeros((rows, 2 * blk), jnp.float32), unroll=slots)

    for f in range(FB_DEV):
        both = gu[last[f]]
        g, u = both[:, :blk], both[:, blk:]
        hb[f] = (g * jax.nn.sigmoid(g) * u).astype(jnp.bfloat16)

    def collect(a):
        @pl.loop(0, dblocks, unroll=4)
        def _(c):
            cols = pl.ds(pl.multiple_of(c * blk, blk), blk)
            total = part[inv[c]]
            for f in range(1, FB_DEV):
                total = total + part[inv[f * dblocks + c]]
            for h in range(PAIR):
                for d in range(line):
                    r = (h * line + d) * per
                    stage[a, h, d, :, cols] = total[r:r + per].astype(jnp.bfloat16)

    chunks = sorted(range(line), key=lambda d: min(2 * d, 2 * (line - 1 - d) + 1))

    def swap(a, base, zt):
        return remote(stage.at[a, 1, zt], xr.at[a, zt], base + zt, base + zt, mate)

    def f_out(zt):
        return remote(zs.at[0, zt], zr.at[0, z], FZ + zt, FZ + z, dev(s, zt))

    def b_out(zt):
        return remote(zs.at[1, zt], zr.at[1, z], BZ + zt, BZ + z, dev(s_prev, zt))

    def o_step(k, _):
        part[k] = jnp.dot(hb[f_of(k)], wd[k], preferred_element_type=jnp.float32)
        return 0
    lax.fori_loop(0, slots, o_step, 0, unroll=slots)
    collect(0)
    for zt in chunks:
        swap(0, FX, zt).start()

    for zt in range(line):
        got(dyg.at[1, zt], DYX + zt)
    pack_dy(1)

    def d_step(k, cur):
        new = lax.dot_general(db[c_of(k)], wd[k], NT, preferred_element_type=jnp.float32)
        cur = cur * keep_of(k) + new
        dh[k] = cur
        return cur
    lax.fori_loop(0, slots, d_step, jnp.zeros((rows, blk), jnp.float32), unroll=slots)

    for f in range(FB_DEV):
        both = gu[last[f]]
        g, u = both[:, :blk], both[:, blk:]
        sg = jax.nn.sigmoid(g)
        dv = dh[last[f]]
        dgu[f, :, :blk] = (dv * u * sg * (1.0 + g * (1.0 - sg))).astype(jnp.bfloat16)
        dgu[f, :, blk:] = (dv * g * sg).astype(jnp.bfloat16)

    def b_step(k, _):
        w = jnp.concatenate([wg[k], wu[k]], axis=1)
        part[k] = lax.dot_general(dgu[f_of(k)], w, NT, preferred_element_type=jnp.float32)
        return 0
    lax.fori_loop(0, slots, b_step, 0, unroll=slots)
    collect(1)
    for zt in chunks:
        swap(1, BX, zt).start()

    def pair_sum(a, zt):
        return stage[a, 0, zt].astype(jnp.float32) + xr[a, zt].astype(jnp.float32)

    for zt in chunks:
        got(xr.at[0, zt], FX + zt)
        zs[0, zt] = pair_sum(0, zt).astype(jnp.bfloat16)

        @pl.when(z != zt)
        def _(zt=zt):
            f_out(zt).start()
    for zt in chunks:
        got(xr.at[1, zt], BX + zt)
        zs[1, zt] = pair_sum(1, zt).astype(jnp.bfloat16)
        b_out(zt).start()

    zr[0, z] = zs[0, z]
    each(offsets, lambda zt: got(zr.at[0, zt], FZ + zt))
    ffn = zr[0, 0].astype(jnp.float32)
    for d in range(1, line):
        ffn = ffn + zr[0, d].astype(jnp.float32)
    for m in range(mb):
        xo = xg[0, z, m].astype(jnp.float32)
        out[0, m] = (xo + ffn[m * tokd:(m + 1) * tokd]).astype(jnp.bfloat16)

    each(offsets, lambda zt: x_line(zt).wait_send())
    x_line(z).wait_send()
    x_mate().wait_send()
    each(offsets, lambda zt: x_relay(zt).wait_send())
    dy_mate().wait_send()
    each(offsets, lambda zt: dy_line(zt).wait_send())
    each(offsets, lambda zt: dy_relay(zt).wait_send())
    dy_back().wait_send()
    gain_back().wait_send()
    for zt in range(line):
        swap(0, FX, zt).wait_send()
        swap(1, BX, zt).wait_send()
    each(offsets, lambda zt: f_out(zt).wait_send())
    got(dyn, DYB)
    got(gn, GNB)
    for zt in range(line):
        got(zr.at[1, zt], BZ + zt)
    gnorm = zr[1, 0].astype(jnp.float32)
    for d in range(1, line):
        gnorm = gnorm + zr[1, d].astype(jnp.float32)
    for m in range(mb):
        xo = cown[m].astype(jnp.float32)
        sc = lax.rsqrt(jnp.mean(xo * xo, axis=-1, keepdims=True) + EPS)
        gg = gn[...] * gnorm[m * tokd:(m + 1) * tokd]
        mixed = jnp.mean(xo * gg, axis=-1, keepdims=True)
        gx = dyn[m].astype(jnp.float32) + sc * gg - xo * (sc * sc * sc) * mixed
        gback[0, m] = gx.astype(jnp.bfloat16)
    for zt in range(line):
        b_out(zt).wait_send()


def on_device(sections, tensors, carry_in, norm_gain, w_gate, w_up, w_down, tile_list, grad_in):
    _, mb, tokd, width = carry_in.shape
    slots, blk = w_gate.shape[1], w_gate.shape[-1]
    line = tensors // PAIR
    per = mb * tokd
    half = line * per
    rows = PAIR * half
    dblocks = width // blk
    bf, f32 = jnp.bfloat16, jnp.float32
    V = pltpu.VMEM
    anyspec = pl.BlockSpec(memory_space=pl.ANY)
    nsem = 8 * line + 2
    parts = pl.pallas_call(
        functools.partial(kernel, sections, tensors),
        out_shape=[jax.ShapeDtypeStruct(carry_in.shape, bf)] * 2,
        in_specs=[pl.BlockSpec(memory_space=pltpu.HBM)] * 7,
        out_specs=[pl.BlockSpec(memory_space=pltpu.VMEM)] * 2,
        scratch_shapes=[
            V((PAIR, line, mb, tokd, width), bf),
            V((PAIR, line, mb, tokd, width), bf),
            V((mb, tokd, width), bf),
            V((1, width), f32),
            V((1, width), f32),
            V((mb, tokd, width), bf),
            V((slots, blk, blk), bf),
            V((slots, blk, blk), bf),
            V((slots, blk, blk), bf),
            V((dblocks, rows, blk), bf),
            V((dblocks, rows, blk), bf),
            V((dblocks, rows, blk), f32),
            V((slots + 1, rows, 2 * blk), f32),
            V((slots + 1, rows, blk), f32),
            V((slots + 1, rows, blk), f32),
            V((FB_DEV, rows, blk), bf),
            V((FB_DEV, rows, 2 * blk), bf),
            V((2, PAIR, line, per, width), bf),
            V((2, line, per, width), bf),
            V((2, line, per, width), bf),
            V((2, line, per, width), bf),
            pltpu.SMEM((1, slots), jnp.int32),
            pltpu.SMEM((FB_DEV * dblocks,), jnp.int32),
            pltpu.SMEM((FB_DEV,), jnp.int32),
            pltpu.SemaphoreType.DMA((7,)),
            pltpu.SemaphoreType.DMA((nsem,)),
            pltpu.SemaphoreType.DMA((nsem,)),
        ],
        compiler_params=pltpu.CompilerParams(
            collective_id=0, has_side_effects=True, vmem_limit_bytes=48 * 1024 * 1024
        ),
    )(*(pltpu.with_memory_space_constraint(v, pltpu.HBM) for v in (tile_list, carry_in, norm_gain, w_gate, w_up, w_down, grad_in)))
    return pl.pallas_call(
        store,
        out_shape=[jax.ShapeDtypeStruct(carry_in.shape, bf)] * 2,
        in_specs=[pl.BlockSpec(memory_space=pltpu.VMEM)] * 2,
        out_specs=[anyspec] * 2,
        scratch_shapes=[pltpu.SemaphoreType.DMA((2,))],
        compiler_params=pltpu.CompilerParams(vmem_limit_bytes=1024 * 1024),
    )(*parts)


def store(a, b, out_a, out_b, sem):
    copies = [
        pltpu.make_async_copy(a, out_a, sem.at[0]),
        pltpu.make_async_copy(b, out_b, sem.at[1]),
    ]
    for c in copies:
        c.start()
    for c in copies:
        c.wait()


def solution(mesh):
    placed = (
        P("section", None, "tensor", None),
        P("section", None),
        P("section", "tensor", None, None),
        P("section", "tensor", None, None),
        P("section", "tensor", None, None),
        P("section", "tensor"),
        P("section", None, "tensor", None),
    )
    return jax.shard_map(
        functools.partial(on_device, mesh.shape["section"], mesh.shape["tensor"]),
        mesh=mesh,
        in_specs=placed,
        out_specs=(P("section", None, "tensor", None), P("section", None, "tensor", None)),
        check_vma=False,
    )
```

```python
import functools

import jax
import jax.numpy as jnp
from jax import lax
from jax.experimental import pallas as pl
from jax.experimental.pallas import tpu as pltpu
from jax.sharding import PartitionSpec as P

FB_DEV = 4
EPS = 1e-05
PAIR = 2
MESH = pl.DeviceIdType.MESH


def kernel(
    sections, tensors,
    tl_h, carry, gain, wg_h, wu_h, wd_h, dy_h,
    out, gback,
    xg, dyg, dyn, gn, gv, cown, wg, wu, wd, nb, db, xs, gu, dh, part, hb, dgu,
    stage, xr, zs, zr, wr, gsum, wdt, wgt, tl, inv, last, lsem, ssem, rsem,
):
    line = tensors // PAIR
    mb, tokd, width = carry.shape[1:]
    per = mb * tokd
    half = line * per
    rows = PAIR * half
    blk = wg.shape[-1]
    slots = wg.shape[0]
    dblocks = width // blk
    s = lax.axis_index("section")
    t = lax.axis_index("tensor")
    z, x = t // PAIR, t % PAIR
    s_next, s_prev = (s + 1) % sections, (s + sections - 1) % sections

    def dev(sec, zt, other=False):
        return (sec, zt * PAIR + ((PAIR - 1 - x) if other else x))

    local = [
        pltpu.make_async_copy(tl_h, tl, lsem.at[6]),
        pltpu.make_async_copy(carry.at[0], cown, lsem.at[5]),
        pltpu.make_async_copy(dy_h.at[0], dyg.at[0, z], lsem.at[0]),
        pltpu.make_async_copy(gain, gv, lsem.at[4]),
        pltpu.make_async_copy(wg_h.at[0], wg, lsem.at[2]),
        pltpu.make_async_copy(wu_h.at[0], wu, lsem.at[3]),
        pltpu.make_async_copy(wd_h.at[0], wd, lsem.at[1]),
    ]
    for c in local:
        c.start()

    offsets = sorted((o for o in range(1 - line, line) if o), key=abs)

    def each(offs, body):
        for o in offs:
            zt = z + o

            @pl.when(jnp.logical_and(zt >= 0, zt < line))
            def _(zt=zt):
                body(zt)

    barrier = pltpu.get_barrier_semaphore()

    def greet(to):
        pl.semaphore_signal(barrier, inc=1, device_id=to, device_id_type=MESH)

    greet(dev(s, z, True))
    greet(dev(s_prev, z))
    greet(dev(s_prev, z, True))

    def greet_line(zt):
        greet(dev(s, zt))
        greet(dev(s_prev, zt))
    each(offsets, greet_line)
    pl.semaphore_wait(barrier, 2 * line + 1)

    def remote(src, dst, si, ri, to):
        return pltpu.make_async_remote_copy(
            src_ref=src, dst_ref=dst, send_sem=ssem.at[si], recv_sem=rsem.at[ri],
            device_id=to, device_id_type=MESH,
        )

    XZ, XX, DYZ, DYX, FX, BX, FZ, BZ = (i * line for i in range(8))
    BW = 8 * line
    DYB, GNB = 9 * line, 9 * line + 1
    mate = dev(s, z, True)

    def x_line(zt):
        return remote(carry.at[0], xg.at[0, z], XZ + zt, XZ + z, dev(s_next, zt))

    def x_mate():
        return remote(carry.at[0], xg.at[1, z], XX + z, XX + z, dev(s_next, z, True))

    def x_relay(zt):
        return remote(xg.at[0, zt], xg.at[1, zt], XX + zt, XX + zt, mate)

    def dy_line(zt):
        return remote(dy_h.at[0], dyg.at[0, z], DYZ + zt, DYZ + z, dev(s, zt))

    def dy_mate():
        return remote(dy_h.at[0], dyg.at[1, z], DYX + z, DYX + z, mate)

    def dy_relay(zt):
        return remote(dyg.at[0, zt], dyg.at[1, zt], DYX + zt, DYX + zt, mate)

    def dy_back():
        return remote(dy_h.at[0], dyn, DYB, DYB, dev(s_prev, z))

    def gain_back():
        return remote(gain, gn, GNB, GNB, dev(s_prev, z))

    def got(dst, ri):
        remote(dst, dst, ri, ri, mate).wait_recv()

    each(offsets, lambda zt: x_line(zt).start())
    x_line(z).start()
    x_mate().start()
    dy_mate().start()

    local[0].wait()
    p = jnp.int32(0)
    for f in range(FB_DEV):
        def cell(i, p, f=f):
            q = f * dblocks + i
            hit = tl[0, jnp.minimum(p, slots - 1)] == q
            inv[q] = jnp.where(hit, p, slots)
            return p + hit.astype(jnp.int32)
        p_new = lax.fori_loop(0, dblocks, cell, p, unroll=4)
        last[f] = jnp.where(p_new > p, p_new - 1, slots)
        p = p_new
    gu[slots] = jnp.zeros((rows, 2 * blk), jnp.float32)
    dh[slots] = jnp.zeros((rows, blk), jnp.float32)
    part[slots] = jnp.zeros((rows, blk), jnp.float32)

    def rows_of(ref, c, h):
        cols = pl.ds(pl.multiple_of(c * blk, blk), blk)
        pieces = []
        for d in range(line):
            for m in range(mb):
                pieces.append(ref[h, d, m, :, cols].astype(jnp.float32))
        return jnp.concatenate(pieces, axis=0)

    def f_of(k):
        return jnp.minimum(tl[0, k] // dblocks, FB_DEV - 1)

    def c_of(k):
        return tl[0, k] % dblocks

    def keep_of(k):
        return (f_of(k) == f_of(jnp.maximum(k - 1, 0))).astype(jnp.float32)

    def square(h):
        def body(c, acc):
            v = rows_of(xg, c, h)
            xs[c, h * half:(h + 1) * half] = v
            return acc + v * v
        return lax.fori_loop(0, dblocks, body, jnp.zeros((half, blk), jnp.float32), unroll=4)

    def pack_dy(h):
        @pl.loop(0, dblocks, unroll=4)
        def _(c):
            db[c, h * half:(h + 1) * half] = rows_of(dyg, c, h).astype(jnp.bfloat16)

    def turn(ref, src, at):
        @pl.loop(0, slots, unroll=8)
        def _(k):
            ref[k, at:at + blk] = src[k].T

    each(offsets, lambda zt: dy_line(zt).start())
    for i, (ref, src, at) in ((6, (wdt, wd, 0)), (4, (wgt, wg, 0)), (5, (wgt, wu, blk))):
        local[i].wait()
        turn(ref, src, at)
    def relay_x(zt):
        got(xg.at[0, zt], XZ + zt)
        x_relay(zt).start()
    each(offsets, relay_x)
    got(xg.at[0, z], XZ + z)
    dy_back().start()
    gain_back().start()
    acc_own = square(0)
    def relay_dy(zt):
        got(dyg.at[0, zt], DYZ + zt)
        dy_relay(zt).start()
    each(offsets, relay_dy)
    for c in local[1:4]:
        c.wait()
    pack_dy(0)
    for zt in range(line):
        got(xg.at[1, zt], XX + zt)
    acc = jnp.concatenate([acc_own, square(1)], axis=0)
    scale = lax.rsqrt(jnp.sum(acc, axis=-1, keepdims=True) / width + EPS)

    @pl.loop(0, dblocks, unroll=4)
    def _(c):
        cols = pl.ds(pl.multiple_of(c * blk, blk), blk)
        nb[c] = (xs[c] * scale * gv[:, cols]).astype(jnp.bfloat16)

    def g_step(k, cur):
        w = jnp.concatenate([wg[k], wu[k]], axis=1)
        new = jnp.dot(nb[c_of(k)], w, preferred_element_type=jnp.float32)
        cur = cur * keep_of(k) + new
        gu[k] = cur
        return cur
    lax.fori_loop(0, slots, g_step, jnp.zeros((rows, 2 * blk), jnp.float32), unroll=slots)

    for f in range(FB_DEV):
        both = gu[last[f]]
        g, u = both[:, :blk], both[:, blk:]
        hb[f] = (g * jax.nn.sigmoid(g) * u).astype(jnp.bfloat16)

    def collect(a):
        @pl.loop(0, dblocks, unroll=4)
        def _(c):
            cols = pl.ds(pl.multiple_of(c * blk, blk), blk)
            total = part[inv[c]]
            for f in range(1, FB_DEV):
                total = total + part[inv[f * dblocks + c]]
            for h in range(PAIR):
                for d in range(line):
                    r = (h * line + d) * per
                    stage[a, h, d, :, cols] = total[r:r + per].astype(jnp.bfloat16)

    chunks = sorted(range(line), key=lambda d: min(2 * d, 2 * (line - 1 - d) + 1))

    def swap(a, base, zt):
        return remote(stage.at[a, 1, zt], xr.at[a, zt], base + zt, base + zt, mate)

    def f_out(zt):
        return remote(zs.at[0, zt], zr.at[0, z], FZ + zt, FZ + z, dev(s, zt))

    def b_out(zt):
        return remote(zs.at[1, zt], zr.at[1, z], BZ + zt, BZ + z, dev(s_prev, zt))

    ends = []
    inner = [zt for zt in chunks if zt not in ends]

    def b_own(zt):
        return remote(stage.at[1, 0, zt], zr.at[1, z], BZ + zt, BZ + z, dev(s_prev, zt))

    def b_other(zt):
        return remote(stage.at[1, 1, zt], wr.at[z], BW + zt, BW + z, dev(s_prev, zt, True))

    def o_step(k, _):
        part[k] = jnp.dot(hb[f_of(k)], wd[k], preferred_element_type=jnp.float32)
        return 0
    lax.fori_loop(0, slots, o_step, 0, unroll=slots)
    collect(0)
    for zt in chunks:
        swap(0, FX, zt).start()

    for zt in range(line):
        got(dyg.at[1, zt], DYX + zt)
    pack_dy(1)

    def d_step(k, cur):
        new = jnp.dot(db[c_of(k)], wdt[k], preferred_element_type=jnp.float32)
        cur = cur * keep_of(k) + new
        dh[k] = cur
        return cur
    lax.fori_loop(0, slots, d_step, jnp.zeros((rows, blk), jnp.float32), unroll=slots)

    for f in range(FB_DEV):
        both = gu[last[f]]
        g, u = both[:, :blk], both[:, blk:]
        sg = jax.nn.sigmoid(g)
        dv = dh[last[f]]
        dgu[f, :, :blk] = (dv * u * sg * (1.0 + g * (1.0 - sg))).astype(jnp.bfloat16)
        dgu[f, :, blk:] = (dv * g * sg).astype(jnp.bfloat16)

    def b_step(k, _):
        part[k] = jnp.dot(dgu[f_of(k)], wgt[k], preferred_element_type=jnp.float32)
        return 0
    lax.fori_loop(0, slots, b_step, 0, unroll=slots)
    collect(1)
    for zt in chunks:
        swap(1, BX, zt).start()

    def pair_sum(a, zt):
        return stage[a, 0, zt].astype(jnp.float32) + xr[a, zt].astype(jnp.float32)

    for zt in chunks:
        got(xr.at[0, zt], FX + zt)
        zs[0, zt] = pair_sum(0, zt).astype(jnp.bfloat16)

        @pl.when(z != zt)
        def _(zt=zt):
            f_out(zt).start()
    for zt in inner:
        got(xr.at[1, zt], BX + zt)
        zs[1, zt] = pair_sum(1, zt).astype(jnp.bfloat16)
        b_out(zt).start()

    zr[0, z] = zs[0, z]
    each(offsets, lambda zt: got(zr.at[0, zt], FZ + zt))
    ffn = zr[0, 0].astype(jnp.float32)
    for d in range(1, line):
        ffn = ffn + zr[0, d].astype(jnp.float32)
    for m in range(mb):
        xo = xg[0, z, m].astype(jnp.float32)
        out[0, m] = (xo + ffn[m * tokd:(m + 1) * tokd]).astype(jnp.bfloat16)

    each(offsets, lambda zt: x_line(zt).wait_send())
    x_line(z).wait_send()
    x_mate().wait_send()
    each(offsets, lambda zt: x_relay(zt).wait_send())
    dy_mate().wait_send()
    each(offsets, lambda zt: dy_line(zt).wait_send())
    each(offsets, lambda zt: dy_relay(zt).wait_send())
    dy_back().wait_send()
    gain_back().wait_send()
    for zt in range(line):
        swap(0, FX, zt).wait_send()
    for zt in inner:
        swap(1, BX, zt).wait_send()
    for zt in ends:
        b_own(zt).wait_send()
        b_other(zt).wait_send()
    each(offsets, lambda zt: f_out(zt).wait_send())
    got(dyn, DYB)
    got(gn, GNB)
    for zt in range(line):
        got(zr.at[1, zt], BZ + zt)
    total = zr[1, 0].astype(jnp.float32)
    for d in range(1, line):
        total = total + zr[1, d].astype(jnp.float32)
    gsum[...] = total

    @pl.when(z < 0)
    def _():
        for zt in range(line):
            got(wr.at[zt], BW + zt)
        total = gsum[...]
        for d in range(line):
            total = total + wr[d].astype(jnp.float32)
        gsum[...] = total
    gnorm = gsum[...]
    for m in range(mb):
        xo = cown[m].astype(jnp.float32)
        sc = lax.rsqrt(jnp.mean(xo * xo, axis=-1, keepdims=True) + EPS)
        gg = gn[...] * gnorm[m * tokd:(m + 1) * tokd]
        mixed = jnp.mean(xo * gg, axis=-1, keepdims=True)
        gx = dyn[m].astype(jnp.float32) + sc * gg - xo * (sc * sc * sc) * mixed
        gback[0, m] = gx.astype(jnp.bfloat16)
    for zt in inner:
        b_out(zt).wait_send()


def on_device(sections, tensors, carry_in, norm_gain, w_gate, w_up, w_down, tile_list, grad_in):
    _, mb, tokd, width = carry_in.shape
    slots, blk = w_gate.shape[1], w_gate.shape[-1]
    line = tensors // PAIR
    per = mb * tokd
    half = line * per
    rows = PAIR * half
    dblocks = width // blk
    bf, f32 = jnp.bfloat16, jnp.float32
    V = pltpu.VMEM
    anyspec = pl.BlockSpec(memory_space=pl.ANY)
    nsem = 9 * line + 2
    parts = pl.pallas_call(
        functools.partial(kernel, sections, tensors),
        out_shape=[jax.ShapeDtypeStruct(carry_in.shape, bf)] * 2,
        in_specs=[pl.BlockSpec(memory_space=pltpu.HBM)] * 7,
        out_specs=[pl.BlockSpec(memory_space=pltpu.VMEM)] * 2,
        scratch_shapes=[
            V((PAIR, line, mb, tokd, width), bf),
            V((PAIR, line, mb, tokd, width), bf),
            V((mb, tokd, width), bf),
            V((1, width), f32),
            V((1, width), f32),
            V((mb, tokd, width), bf),
            V((slots, blk, blk), bf),
            V((slots, blk, blk), bf),
            V((slots, blk, blk), bf),
            V((dblocks, rows, blk), bf),
            V((dblocks, rows, blk), bf),
            V((dblocks, rows, blk), f32),
            V((slots + 1, rows, 2 * blk), f32),
            V((slots + 1, rows, blk), f32),
            V((slots + 1, rows, blk), f32),
            V((FB_DEV, rows, blk), bf),
            V((FB_DEV, rows, 2 * blk), bf),
            V((2, PAIR, line, per, width), bf),
            V((2, line, per, width), bf),
            V((2, line, per, width), bf),
            V((2, line, per, width), bf),
            V((line, per, width), bf),
            V((per, width), f32),
            V((slots, blk, blk), bf),
            V((slots, 2 * blk, blk), bf),
            pltpu.SMEM((1, slots), jnp.int32),
            pltpu.SMEM((FB_DEV * dblocks,), jnp.int32),
            pltpu.SMEM((FB_DEV,), jnp.int32),
            pltpu.SemaphoreType.DMA((7,)),
            pltpu.SemaphoreType.DMA((nsem,)),
            pltpu.SemaphoreType.DMA((nsem,)),
        ],
        compiler_params=pltpu.CompilerParams(
            collective_id=0, has_side_effects=True, vmem_limit_bytes=48 * 1024 * 1024
        ),
    )(*(pltpu.with_memory_space_constraint(v, pltpu.HBM) for v in (tile_list, carry_in, norm_gain, w_gate, w_up, w_down, grad_in)))
    return pl.pallas_call(
        store,
        out_shape=[jax.ShapeDtypeStruct(carry_in.shape, bf)] * 2,
        in_specs=[pl.BlockSpec(memory_space=pltpu.VMEM)] * 2,
        out_specs=[anyspec] * 2,
        scratch_shapes=[pltpu.SemaphoreType.DMA((2,))],
        compiler_params=pltpu.CompilerParams(vmem_limit_bytes=1024 * 1024),
    )(*parts)


def store(a, b, out_a, out_b, sem):
    copies = [
        pltpu.make_async_copy(a, out_a, sem.at[0]),
        pltpu.make_async_copy(b, out_b, sem.at[1]),
    ]
    for c in copies:
        c.start()
    for c in copies:
        c.wait()


def solution(mesh):
    placed = (
        P("section", None, "tensor", None),
        P("section", None),
        P("section", "tensor", None, None),
        P("section", "tensor", None, None),
        P("section", "tensor", None, None),
        P("section", "tensor"),
        P("section", None, "tensor", None),
    )
    return jax.shard_map(
        functools.partial(on_device, mesh.shape["section"], mesh.shape["tensor"]),
        mesh=mesh,
        in_specs=placed,
        out_specs=(P("section", None, "tensor", None), P("section", None, "tensor", None)),
        check_vma=False,
    )
```

```python
import functools

import jax
import jax.numpy as jnp
from jax import lax
from jax.experimental import pallas as pl
from jax.experimental.pallas import tpu as pltpu
from jax.sharding import PartitionSpec as P

FB_DEV = 4
EPS = 1e-05
PAIR = 2
MESH = pl.DeviceIdType.MESH


def kernel(
    sections, tensors,
    tl_h, carry, gain, wg_h, wu_h, wd_h, dy_h,
    out, gback,
    xg, dyg, dyn, gn, gv, cown, wg, wu, wd, nb, db, xs, gu, dh, part, hb, dgu,
    stage, xr, zs, zr, wdt, wgt, tl, inv, last, lsem, ssem, rsem,
):
    line = tensors // PAIR
    mb, tokd, width = carry.shape[1:]
    per = mb * tokd
    half = line * per
    rows = PAIR * half
    blk = wg.shape[-1]
    slots = wg.shape[0]
    dblocks = width // blk
    s = lax.axis_index("section")
    t = lax.axis_index("tensor")
    z, x = t // PAIR, t % PAIR
    s_next, s_prev = (s + 1) % sections, (s + sections - 1) % sections

    def dev(sec, zt, other=False):
        return (sec, zt * PAIR + ((PAIR - 1 - x) if other else x))

    local = [
        pltpu.make_async_copy(tl_h, tl, lsem.at[6]),
        pltpu.make_async_copy(carry.at[0], cown, lsem.at[5]),
        pltpu.make_async_copy(dy_h.at[0], dyg.at[0, z], lsem.at[0]),
        pltpu.make_async_copy(gain, gv, lsem.at[4]),
        pltpu.make_async_copy(wg_h.at[0], wg, lsem.at[2]),
        pltpu.make_async_copy(wu_h.at[0], wu, lsem.at[3]),
        pltpu.make_async_copy(wd_h.at[0], wd, lsem.at[1]),
    ]
    for c in local:
        c.start()

    offsets = sorted((o for o in range(1 - line, line) if o), key=abs)

    def each(offs, body):
        for o in offs:
            zt = z + o

            @pl.when(jnp.logical_and(zt >= 0, zt < line))
            def _(zt=zt):
                body(zt)

    barrier = pltpu.get_barrier_semaphore()

    def greet(to):
        pl.semaphore_signal(barrier, inc=1, device_id=to, device_id_type=MESH)

    greet(dev(s, z, True))
    greet(dev(s_prev, z))
    greet(dev(s_prev, z, True))

    def greet_line(zt):
        greet(dev(s, zt))
        greet(dev(s_prev, zt))
    each(offsets, greet_line)
    pl.semaphore_wait(barrier, 2 * line + 1)

    def remote(src, dst, si, ri, to):
        return pltpu.make_async_remote_copy(
            src_ref=src, dst_ref=dst, send_sem=ssem.at[si], recv_sem=rsem.at[ri],
            device_id=to, device_id_type=MESH,
        )

    XZ, DYZ, FX, BX, FZ = (i * line for i in range(5))
    XX, DYX, BZ, DYB, GNB = (5 * line + i for i in range(5))
    SX, SDY, SW, SB, SG, SF = range(6)
    mate = dev(s, z, True)

    def x_line(zt):
        return remote(carry.at[0], xg.at[0, z], SX, XZ + z, dev(s_next, zt))

    def x_mate():
        return remote(carry.at[0], xg.at[1, z], SX, XX, dev(s_next, z, True))

    def x_relay(zt):
        return remote(xg.at[0, zt], xg.at[1, zt], SX, XX, mate)

    def dy_line(zt):
        return remote(dy_h.at[0], dyg.at[0, z], SDY, DYZ + z, dev(s, zt))

    def dy_mate():
        return remote(dy_h.at[0], dyg.at[1, z], SDY, DYX, mate)

    def dy_relay(zt):
        return remote(dyg.at[0, zt], dyg.at[1, zt], SDY, DYX, mate)

    def dy_back():
        return remote(dy_h.at[0], dyn, SDY, DYB, dev(s_prev, z))

    def gain_back():
        return remote(gain, gn, SG, GNB, dev(s_prev, z))

    def got(dst, ri):
        remote(dst, dst, 0, ri, mate).wait_recv()

    def gone(src, si):
        remote(src, src, si, 0, mate).wait_send()

    each(offsets, lambda zt: x_line(zt).start())
    x_line(z).start()
    x_mate().start()
    dy_mate().start()

    local[0].wait()
    p = jnp.int32(0)
    for f in range(FB_DEV):
        def cell(i, p, f=f):
            q = f * dblocks + i
            hit = tl[0, jnp.minimum(p, slots - 1)] == q
            inv[q] = jnp.where(hit, p, slots)
            return p + hit.astype(jnp.int32)
        p_new = lax.fori_loop(0, dblocks, cell, p, unroll=4)
        last[f] = jnp.where(p_new > p, p_new - 1, slots)
        p = p_new
    gu[slots] = jnp.zeros((rows, 2 * blk), jnp.float32)
    dh[slots] = jnp.zeros((rows, blk), jnp.float32)
    part[slots] = jnp.zeros((rows, blk), jnp.float32)

    def rows_of(ref, c, h):
        cols = pl.ds(pl.multiple_of(c * blk, blk), blk)
        pieces = []
        for d in range(line):
            for m in range(mb):
                pieces.append(ref[h, d, m, :, cols].astype(jnp.float32))
        return jnp.concatenate(pieces, axis=0)

    def f_of(k):
        return jnp.minimum(tl[0, k] // dblocks, FB_DEV - 1)

    def c_of(k):
        return tl[0, k] % dblocks

    def keep_of(k):
        return (f_of(k) == f_of(jnp.maximum(k - 1, 0))).astype(jnp.float32)

    def square(h):
        def body(c, acc):
            v = rows_of(xg, c, h)
            xs[c, h * half:(h + 1) * half] = v
            return acc + v * v
        return lax.fori_loop(0, dblocks, body, jnp.zeros((half, blk), jnp.float32), unroll=4)

    def pack_dy(h):
        @pl.loop(0, dblocks, unroll=4)
        def _(c):
            db[c, h * half:(h + 1) * half] = rows_of(dyg, c, h).astype(jnp.bfloat16)

    def turn(ref, src, at):
        @pl.loop(0, slots, unroll=8)
        def _(k):
            ref[k, at:at + blk] = src[k].T

    each(offsets, lambda zt: dy_line(zt).start())
    for i, (ref, src, at) in ((6, (wdt, wd, 0)), (4, (wgt, wg, 0)), (5, (wgt, wu, blk))):
        local[i].wait()
        turn(ref, src, at)
    def relay_x(zt):
        got(xg.at[0, zt], XZ + zt)
        x_relay(zt).start()
    each(offsets, relay_x)
    got(xg.at[0, z], XZ + z)
    dy_back().start()
    gain_back().start()
    acc_own = square(0)
    def relay_dy(zt):
        got(dyg.at[0, zt], DYZ + zt)
        dy_relay(zt).start()
    each(offsets, relay_dy)
    for c in local[1:4]:
        c.wait()
    pack_dy(0)
    got(xg.at[1], XX)
    acc = jnp.concatenate([acc_own, square(1)], axis=0)
    scale = lax.rsqrt(jnp.sum(acc, axis=-1, keepdims=True) / width + EPS)

    @pl.loop(0, dblocks, unroll=4)
    def _(c):
        cols = pl.ds(pl.multiple_of(c * blk, blk), blk)
        nb[c] = (xs[c] * scale * gv[:, cols]).astype(jnp.bfloat16)

    def g_step(k, cur):
        w = jnp.concatenate([wg[k], wu[k]], axis=1)
        new = jnp.dot(nb[c_of(k)], w, preferred_element_type=jnp.float32)
        cur = cur * keep_of(k) + new
        gu[k] = cur
        return cur
    lax.fori_loop(0, slots, g_step, jnp.zeros((rows, 2 * blk), jnp.float32), unroll=slots)

    for f in range(FB_DEV):
        both = gu[last[f]]
        g, u = both[:, :blk], both[:, blk:]
        hb[f] = (g * jax.nn.sigmoid(g) * u).astype(jnp.bfloat16)

    def collect(a):
        @pl.loop(0, dblocks, unroll=4)
        def _(c):
            cols = pl.ds(pl.multiple_of(c * blk, blk), blk)
            total = part[inv[c]]
            for f in range(1, FB_DEV):
                total = total + part[inv[f * dblocks + c]]
            for h in range(PAIR):
                for d in range(line):
                    r = (h * line + d) * per
                    stage[a, h, d, :, cols] = total[r:r + per].astype(jnp.bfloat16)

    def away(body):
        @pl.when(2 * z < line)
        def _():
            for zt in reversed(range(line)):
                @pl.when(z != zt)
                def _(zt=zt):
                    body(zt)

        @pl.when(2 * z >= line)
        def _():
            for zt in range(line):
                @pl.when(z != zt)
                def _(zt=zt):
                    body(zt)

    def own(body):
        for zt in range(line):
            @pl.when(z == zt)
            def _(zt=zt):
                body(zt)

    def swap(a, base, zt):
        return remote(stage.at[a, 1, zt], xr.at[a, zt], SW, base + zt, mate)

    def f_out(zt):
        return remote(zs.at[0, zt], zr.at[0, z], SF + zt, FZ + z, dev(s, zt))

    def b_out(zt):
        return remote(zs.at[1, zt], zr.at[1, z], SB, BZ, dev(s_prev, zt))

    def o_step(k, _):
        part[k] = jnp.dot(hb[f_of(k)], wd[k], preferred_element_type=jnp.float32)
        return 0
    lax.fori_loop(0, slots, o_step, 0, unroll=slots)
    collect(0)
    away(lambda zt: swap(0, FX, zt).start())

    got(dyg.at[1], DYX)
    pack_dy(1)

    def d_step(k, cur):
        new = jnp.dot(db[c_of(k)], wdt[k], preferred_element_type=jnp.float32)
        cur = cur * keep_of(k) + new
        dh[k] = cur
        return cur
    lax.fori_loop(0, slots, d_step, jnp.zeros((rows, blk), jnp.float32), unroll=slots)

    for f in range(FB_DEV):
        both = gu[last[f]]
        g, u = both[:, :blk], both[:, blk:]
        sg = jax.nn.sigmoid(g)
        dv = dh[last[f]]
        dgu[f, :, :blk] = (dv * u * sg * (1.0 + g * (1.0 - sg))).astype(jnp.bfloat16)
        dgu[f, :, blk:] = (dv * g * sg).astype(jnp.bfloat16)

    def b_step(k, _):
        part[k] = jnp.dot(dgu[f_of(k)], wgt[k], preferred_element_type=jnp.float32)
        return 0
    lax.fori_loop(0, slots, b_step, 0, unroll=slots)
    collect(1)
    away(lambda zt: swap(1, BX, zt).start())
    swap(1, BX, z).start()
    swap(0, FX, z).start()

    def pair_sum(a, zt):
        return stage[a, 0, zt].astype(jnp.float32) + xr[a, zt].astype(jnp.float32)

    def f_send(zt):
        got(xr.at[0, zt], FX + zt)
        zs[0, zt] = pair_sum(0, zt).astype(jnp.bfloat16)
        f_out(zt).start()
    away(f_send)
    def b_send(zt):
        got(xr.at[1, zt], BX + zt)
        zs[1, zt] = pair_sum(1, zt).astype(jnp.bfloat16)
        b_out(zt).start()
    away(b_send)
    own(b_send)
    def f_keep(zt):
        got(xr.at[0, zt], FX + zt)
        zr[0, zt] = pair_sum(0, zt).astype(jnp.bfloat16)
    own(f_keep)
    each(offsets, lambda zt: got(zr.at[0, zt], FZ + zt))
    ffn = zr[0, 0].astype(jnp.float32)
    for d in range(1, line):
        ffn = ffn + zr[0, d].astype(jnp.float32)
    for m in range(mb):
        xo = xg[0, z, m].astype(jnp.float32)
        out[0, m] = (xo + ffn[m * tokd:(m + 1) * tokd]).astype(jnp.bfloat16)

    gone(xg, SX)
    gone(dyg, SDY)
    gone(gain, SG)
    gone(xr, SW)
    each(offsets, lambda zt: f_out(zt).wait_send())
    got(dyn, DYB)
    got(gn, GNB)
    got(zr.at[1], BZ)
    gnorm = zr[1, 0].astype(jnp.float32)
    for d in range(1, line):
        gnorm = gnorm + zr[1, d].astype(jnp.float32)
    for m in range(mb):
        xo = cown[m].astype(jnp.float32)
        sc = lax.rsqrt(jnp.mean(xo * xo, axis=-1, keepdims=True) + EPS)
        gg = gn[...] * gnorm[m * tokd:(m + 1) * tokd]
        mixed = jnp.mean(xo * gg, axis=-1, keepdims=True)
        gx = dyn[m].astype(jnp.float32) + sc * gg - xo * (sc * sc * sc) * mixed
        gback[0, m] = gx.astype(jnp.bfloat16)
    gone(zs.at[1], SB)


def on_device(sections, tensors, carry_in, norm_gain, w_gate, w_up, w_down, tile_list, grad_in):
    _, mb, tokd, width = carry_in.shape
    slots, blk = w_gate.shape[1], w_gate.shape[-1]
    line = tensors // PAIR
    per = mb * tokd
    half = line * per
    rows = PAIR * half
    dblocks = width // blk
    bf, f32 = jnp.bfloat16, jnp.float32
    V = pltpu.VMEM
    anyspec = pl.BlockSpec(memory_space=pl.ANY)
    parts = pl.pallas_call(
        functools.partial(kernel, sections, tensors),
        out_shape=[jax.ShapeDtypeStruct(carry_in.shape, bf)] * 2,
        in_specs=[pl.BlockSpec(memory_space=pltpu.HBM)] * 7,
        out_specs=[pl.BlockSpec(memory_space=pltpu.VMEM)] * 2,
        scratch_shapes=[
            V((PAIR, line, mb, tokd, width), bf),
            V((PAIR, line, mb, tokd, width), bf),
            V((mb, tokd, width), bf),
            V((1, width), f32),
            V((1, width), f32),
            V((mb, tokd, width), bf),
            V((slots, blk, blk), bf),
            V((slots, blk, blk), bf),
            V((slots, blk, blk), bf),
            V((dblocks, rows, blk), bf),
            V((dblocks, rows, blk), bf),
            V((dblocks, rows, blk), f32),
            V((slots + 1, rows, 2 * blk), f32),
            V((slots + 1, rows, blk), f32),
            V((slots + 1, rows, blk), f32),
            V((FB_DEV, rows, blk), bf),
            V((FB_DEV, rows, 2 * blk), bf),
            V((2, PAIR, line, per, width), bf),
            V((2, line, per, width), bf),
            V((2, line, per, width), bf),
            V((2, line, per, width), bf),
            V((slots, blk, blk), bf),
            V((slots, 2 * blk, blk), bf),
            pltpu.SMEM((1, slots), jnp.int32),
            pltpu.SMEM((FB_DEV * dblocks,), jnp.int32),
            pltpu.SMEM((FB_DEV,), jnp.int32),
            pltpu.SemaphoreType.DMA((7,)),
            pltpu.SemaphoreType.DMA((5 + line,)),
            pltpu.SemaphoreType.DMA((5 * line + 5,)),
        ],
        compiler_params=pltpu.CompilerParams(
            collective_id=0, has_side_effects=True, vmem_limit_bytes=48 * 1024 * 1024
        ),
    )(*(pltpu.with_memory_space_constraint(v, pltpu.HBM) for v in (tile_list, carry_in, norm_gain, w_gate, w_up, w_down, grad_in)))
    return pl.pallas_call(
        store,
        out_shape=[jax.ShapeDtypeStruct(carry_in.shape, bf)] * 2,
        in_specs=[pl.BlockSpec(memory_space=pltpu.VMEM)] * 2,
        out_specs=[anyspec] * 2,
        scratch_shapes=[pltpu.SemaphoreType.DMA((2,))],
        compiler_params=pltpu.CompilerParams(vmem_limit_bytes=1024 * 1024),
    )(*parts)


def store(a, b, out_a, out_b, sem):
    copies = [
        pltpu.make_async_copy(a, out_a, sem.at[0]),
        pltpu.make_async_copy(b, out_b, sem.at[1]),
    ]
    for c in copies:
        c.start()
    for c in copies:
        c.wait()


def solution(mesh):
    placed = (
        P("section", None, "tensor", None),
        P("section", None),
        P("section", "tensor", None, None),
        P("section", "tensor", None, None),
        P("section", "tensor", None, None),
        P("section", "tensor"),
        P("section", None, "tensor", None),
    )
    return jax.shard_map(
        functools.partial(on_device, mesh.shape["section"], mesh.shape["tensor"]),
        mesh=mesh,
        in_specs=placed,
        out_specs=(P("section", None, "tensor", None), P("section", None, "tensor", None)),
        check_vma=False,
    )
```

```python
import functools

import jax
import jax.numpy as jnp
from jax import lax
from jax.experimental import pallas as pl
from jax.experimental.pallas import tpu as pltpu
from jax.sharding import PartitionSpec as P

FB_DEV = 4
EPS = 1e-05
PAIR = 2
MESH = pl.DeviceIdType.MESH


def kernel(
    sections, tensors,
    tl_h, carry, gain, wg_h, wu_h, wd_h, dy_h,
    out, gback,
    xg, dyg, dyn, gn, gv, cown, wg, wu, wd, nb, db, xs, gu, dh, part, hb, dgu,
    stage, xr, zs, zr, wdt, wgt, tl, inv, last, lsem, ssem, rsem,
):
    line = tensors // PAIR
    mb, tokd, width = carry.shape[1:]
    per = mb * tokd
    half = line * per
    rows = PAIR * half
    blk = wg.shape[-1]
    slots = wg.shape[0]
    dblocks = width // blk
    s = lax.axis_index("section")
    t = lax.axis_index("tensor")
    z, x = t // PAIR, t % PAIR
    s_next, s_prev = (s + 1) % sections, (s + sections - 1) % sections

    def dev(sec, zt, other=False):
        return (sec, zt * PAIR + ((PAIR - 1 - x) if other else x))

    local = [
        pltpu.make_async_copy(tl_h, tl, lsem.at[6]),
        pltpu.make_async_copy(carry.at[0], cown, lsem.at[5]),
        pltpu.make_async_copy(dy_h.at[0], dyg.at[0, z], lsem.at[0]),
        pltpu.make_async_copy(gain, gv, lsem.at[4]),
        pltpu.make_async_copy(wg_h.at[0], wg, lsem.at[2]),
        pltpu.make_async_copy(wu_h.at[0], wu, lsem.at[3]),
        pltpu.make_async_copy(wd_h.at[0], wd, lsem.at[1]),
    ]
    for c in local:
        c.start()

    offsets = sorted((o for o in range(1 - line, line) if o), key=abs)

    def each(offs, body):
        for o in offs:
            zt = z + o

            @pl.when(jnp.logical_and(zt >= 0, zt < line))
            def _(zt=zt):
                body(zt)

    barrier = pltpu.get_barrier_semaphore()

    def greet(to):
        pl.semaphore_signal(barrier, inc=1, device_id=to, device_id_type=MESH)

    greet(dev(s, z, True))
    greet(dev(s_prev, z))
    greet(dev(s_prev, z, True))

    def greet_line(zt):
        greet(dev(s, zt))
        greet(dev(s_prev, zt))
    each(offsets, greet_line)
    pl.semaphore_wait(barrier, 2 * line + 1)

    def remote(src, dst, si, ri, to):
        return pltpu.make_async_remote_copy(
            src_ref=src, dst_ref=dst, send_sem=ssem.at[si], recv_sem=rsem.at[ri],
            device_id=to, device_id_type=MESH,
        )

    XZ, DYZ, FX, BX, FZ = (i * line for i in range(5))
    XX, DYX, BZ, DYB, GNB = (5 * line + i for i in range(5))
    SX, SDY, SW, SB, SG, SF = range(6)
    mate = dev(s, z, True)

    def x_line(zt):
        return remote(carry.at[0], xg.at[0, z], SX, XZ + z, dev(s_next, zt))

    def x_mate():
        return remote(carry.at[0], xg.at[1, z], SX, XX, dev(s_next, z, True))

    def x_relay(zt):
        return remote(xg.at[0, zt], xg.at[1, zt], SX, XX, mate)

    def dy_line(zt):
        return remote(dy_h.at[0], dyg.at[0, z], SDY, DYZ + z, dev(s, zt))

    def dy_mate():
        return remote(dy_h.at[0], dyg.at[1, z], SDY, DYX, mate)

    def dy_relay(zt):
        return remote(dyg.at[0, zt], dyg.at[1, zt], SDY, DYX, mate)

    def dy_back():
        return remote(dy_h.at[0], dyn, SDY, DYB, dev(s_prev, z))

    def gain_back():
        return remote(gain, gn, SG, GNB, dev(s_prev, z))

    def got(dst, ri):
        remote(dst, dst, 0, ri, mate).wait_recv()

    def gone(src, si):
        remote(src, src, si, 0, mate).wait_send()

    each(offsets, lambda zt: x_line(zt).start())
    x_line(z).start()
    x_mate().start()
    dy_mate().start()

    local[0].wait()
    p = jnp.int32(0)
    for f in range(FB_DEV):
        def cell(i, p, f=f):
            q = f * dblocks + i
            hit = tl[0, jnp.minimum(p, slots - 1)] == q
            inv[q] = jnp.where(hit, p, slots)
            return p + hit.astype(jnp.int32)
        p_new = lax.fori_loop(0, dblocks, cell, p, unroll=4)
        last[f] = jnp.where(p_new > p, p_new - 1, slots)
        p = p_new
    gu[slots] = jnp.zeros((rows, 2 * blk), jnp.float32)
    dh[slots] = jnp.zeros((rows, blk), jnp.float32)
    part[slots] = jnp.zeros((rows, blk), jnp.float32)

    def rows_of(ref, c, h):
        cols = pl.ds(pl.multiple_of(c * blk, blk), blk)
        pieces = []
        for d in range(line):
            for m in range(mb):
                pieces.append(ref[h, d, m, :, cols].astype(jnp.float32))
        return jnp.concatenate(pieces, axis=0)

    def f_of(k):
        return jnp.minimum(tl[0, k] // dblocks, FB_DEV - 1)

    def c_of(k):
        return tl[0, k] % dblocks

    def keep_of(k):
        return (f_of(k) == f_of(jnp.maximum(k - 1, 0))).astype(jnp.float32)

    def square(h):
        def body(c, acc):
            v = rows_of(xg, c, h)
            xs[c, h * half:(h + 1) * half] = v
            return acc + v * v
        return lax.fori_loop(0, dblocks, body, jnp.zeros((half, blk), jnp.float32), unroll=4)

    def norm(h):
        scale = lax.rsqrt(jnp.sum(square(h), axis=-1, keepdims=True) / width + EPS)

        @pl.loop(0, dblocks, unroll=4)
        def _(c):
            cols = pl.ds(pl.multiple_of(c * blk, blk), blk)
            mine = slice(h * half, (h + 1) * half)
            nb[c, mine] = (xs[c, mine] * scale * gv[:, cols]).astype(jnp.bfloat16)

    def pack_dy(h):
        @pl.loop(0, dblocks, unroll=4)
        def _(c):
            db[c, h * half:(h + 1) * half] = rows_of(dyg, c, h).astype(jnp.bfloat16)

    def turn(ref, src, at):
        @pl.loop(0, slots, unroll=8)
        def _(k):
            ref[k, at:at + blk] = src[k].T

    for i, (ref, src, at) in ((6, (wdt, wd, 0)), (4, (wgt, wg, 0)), (5, (wgt, wu, blk))):
        local[i].wait()
        turn(ref, src, at)
    each(offsets, lambda zt: dy_line(zt).start())
    def relay_x(zt):
        got(xg.at[0, zt], XZ + zt)
        x_relay(zt).start()
    each(offsets, relay_x)
    got(xg.at[0, z], XZ + z)
    dy_back().start()
    gain_back().start()
    local[3].wait()
    norm(0)
    def relay_dy(zt):
        got(dyg.at[0, zt], DYZ + zt)
        dy_relay(zt).start()
    each(offsets, relay_dy)
    for c in local[1:3]:
        c.wait()
    pack_dy(0)
    got(xg.at[1], XX)
    norm(1)

    def g_step(k, cur):
        w = jnp.concatenate([wg[k], wu[k]], axis=1)
        new = jnp.dot(nb[c_of(k)], w, preferred_element_type=jnp.float32)
        cur = cur * keep_of(k) + new
        gu[k] = cur
        return cur
    lax.fori_loop(0, slots, g_step, jnp.zeros((rows, 2 * blk), jnp.float32), unroll=slots)

    for f in range(FB_DEV):
        both = gu[last[f]]
        g, u = both[:, :blk], both[:, blk:]
        hb[f] = (g * jax.nn.sigmoid(g) * u).astype(jnp.bfloat16)

    def collect(a, h):
        @pl.loop(0, dblocks, unroll=4)
        def _(c):
            cols = pl.ds(pl.multiple_of(c * blk, blk), blk)
            mine = pl.ds(h * half, half)
            total = part[inv[c], mine]
            for f in range(1, FB_DEV):
                total = total + part[inv[f * dblocks + c], mine]
            for d in range(line):
                stage[a, h, d, :, cols] = total[d * per:(d + 1) * per].astype(jnp.bfloat16)

    def away(body):
        @pl.when(2 * z < line)
        def _():
            for zt in reversed(range(line)):
                @pl.when(z != zt)
                def _(zt=zt):
                    body(zt)

        @pl.when(2 * z >= line)
        def _():
            for zt in range(line):
                @pl.when(z != zt)
                def _(zt=zt):
                    body(zt)

    def own(body):
        for zt in range(line):
            @pl.when(z == zt)
            def _(zt=zt):
                body(zt)

    def swap(a, base, zt):
        return remote(stage.at[a, 1, zt], xr.at[a, zt], SW, base + zt, mate)

    def f_out(zt):
        return remote(zs.at[0, zt], zr.at[0, z], SF + zt, FZ + z, dev(s, zt))

    def b_out(zt):
        return remote(zs.at[1, zt], zr.at[1, z], SB, BZ, dev(s_prev, zt))

    def o_step(k, _):
        part[k] = jnp.dot(hb[f_of(k)], wd[k], preferred_element_type=jnp.float32)
        return 0
    lax.fori_loop(0, slots, o_step, 0, unroll=slots)
    collect(0, 1)
    away(lambda zt: swap(0, FX, zt).start())
    collect(0, 0)

    got(dyg.at[1], DYX)
    pack_dy(1)

    def d_step(k, cur):
        new = jnp.dot(db[c_of(k)], wdt[k], preferred_element_type=jnp.float32)
        cur = cur * keep_of(k) + new
        dh[k] = cur
        return cur
    lax.fori_loop(0, slots, d_step, jnp.zeros((rows, blk), jnp.float32), unroll=slots)

    for f in range(FB_DEV):
        both = gu[last[f]]
        g, u = both[:, :blk], both[:, blk:]
        sg = jax.nn.sigmoid(g)
        dv = dh[last[f]]
        dgu[f, :, :blk] = (dv * u * sg * (1.0 + g * (1.0 - sg))).astype(jnp.bfloat16)
        dgu[f, :, blk:] = (dv * g * sg).astype(jnp.bfloat16)

    def b_step(k, _):
        part[k] = jnp.dot(dgu[f_of(k)], wgt[k], preferred_element_type=jnp.float32)
        return 0
    lax.fori_loop(0, slots, b_step, 0, unroll=slots)
    collect(1, 1)
    away(lambda zt: swap(1, BX, zt).start())
    swap(1, BX, z).start()
    swap(0, FX, z).start()
    collect(1, 0)

    def pair_sum(a, zt):
        return stage[a, 0, zt].astype(jnp.float32) + xr[a, zt].astype(jnp.float32)

    def f_send(zt):
        got(xr.at[0, zt], FX + zt)
        zs[0, zt] = pair_sum(0, zt).astype(jnp.bfloat16)
        f_out(zt).start()
    away(f_send)
    def b_send(zt):
        got(xr.at[1, zt], BX + zt)
        zs[1, zt] = pair_sum(1, zt).astype(jnp.bfloat16)
        b_out(zt).start()
    away(b_send)
    own(b_send)
    def f_keep(zt):
        got(xr.at[0, zt], FX + zt)
        zr[0, zt] = pair_sum(0, zt).astype(jnp.bfloat16)
    own(f_keep)
    each(offsets, lambda zt: got(zr.at[0, zt], FZ + zt))
    ffn = zr[0, 0].astype(jnp.float32)
    for d in range(1, line):
        ffn = ffn + zr[0, d].astype(jnp.float32)
    for m in range(mb):
        xo = xg[0, z, m].astype(jnp.float32)
        out[0, m] = (xo + ffn[m * tokd:(m + 1) * tokd]).astype(jnp.bfloat16)

    gone(xg, SX)
    gone(dyg, SDY)
    gone(gain, SG)
    gone(xr, SW)
    each(offsets, lambda zt: f_out(zt).wait_send())
    got(dyn, DYB)
    got(gn, GNB)
    got(zr.at[1], BZ)
    gnorm = zr[1, 0].astype(jnp.float32)
    for d in range(1, line):
        gnorm = gnorm + zr[1, d].astype(jnp.float32)
    for m in range(mb):
        xo = cown[m].astype(jnp.float32)
        sc = lax.rsqrt(jnp.mean(xo * xo, axis=-1, keepdims=True) + EPS)
        gg = gn[...] * gnorm[m * tokd:(m + 1) * tokd]
        mixed = jnp.mean(xo * gg, axis=-1, keepdims=True)
        gx = dyn[m].astype(jnp.float32) + sc * gg - xo * (sc * sc * sc) * mixed
        gback[0, m] = gx.astype(jnp.bfloat16)
    gone(zs.at[1], SB)


def on_device(sections, tensors, carry_in, norm_gain, w_gate, w_up, w_down, tile_list, grad_in):
    _, mb, tokd, width = carry_in.shape
    slots, blk = w_gate.shape[1], w_gate.shape[-1]
    line = tensors // PAIR
    per = mb * tokd
    half = line * per
    rows = PAIR * half
    dblocks = width // blk
    bf, f32 = jnp.bfloat16, jnp.float32
    V = pltpu.VMEM
    anyspec = pl.BlockSpec(memory_space=pl.ANY)
    parts = pl.pallas_call(
        functools.partial(kernel, sections, tensors),
        out_shape=[jax.ShapeDtypeStruct(carry_in.shape, bf)] * 2,
        in_specs=[pl.BlockSpec(memory_space=pltpu.HBM)] * 7,
        out_specs=[pl.BlockSpec(memory_space=pltpu.VMEM)] * 2,
        scratch_shapes=[
            V((PAIR, line, mb, tokd, width), bf),
            V((PAIR, line, mb, tokd, width), bf),
            V((mb, tokd, width), bf),
            V((1, width), f32),
            V((1, width), f32),
            V((mb, tokd, width), bf),
            V((slots, blk, blk), bf),
            V((slots, blk, blk), bf),
            V((slots, blk, blk), bf),
            V((dblocks, rows, blk), bf),
            V((dblocks, rows, blk), bf),
            V((dblocks, rows, blk), f32),
            V((slots + 1, rows, 2 * blk), f32),
            V((slots + 1, rows, blk), f32),
            V((slots + 1, rows, blk), f32),
            V((FB_DEV, rows, blk), bf),
            V((FB_DEV, rows, 2 * blk), bf),
            V((2, PAIR, line, per, width), bf),
            V((2, line, per, width), bf),
            V((2, line, per, width), bf),
            V((2, line, per, width), bf),
            V((slots, blk, blk), bf),
            V((slots, 2 * blk, blk), bf),
            pltpu.SMEM((1, slots), jnp.int32),
            pltpu.SMEM((FB_DEV * dblocks,), jnp.int32),
            pltpu.SMEM((FB_DEV,), jnp.int32),
            pltpu.SemaphoreType.DMA((7,)),
            pltpu.SemaphoreType.DMA((5 + line,)),
            pltpu.SemaphoreType.DMA((5 * line + 5,)),
        ],
        compiler_params=pltpu.CompilerParams(
            collective_id=0, has_side_effects=True, vmem_limit_bytes=48 * 1024 * 1024
        ),
    )(*(pltpu.with_memory_space_constraint(v, pltpu.HBM) for v in (tile_list, carry_in, norm_gain, w_gate, w_up, w_down, grad_in)))
    return pl.pallas_call(
        store,
        out_shape=[jax.ShapeDtypeStruct(carry_in.shape, bf)] * 2,
        in_specs=[pl.BlockSpec(memory_space=pltpu.VMEM)] * 2,
        out_specs=[anyspec] * 2,
        scratch_shapes=[pltpu.SemaphoreType.DMA((2,))],
        compiler_params=pltpu.CompilerParams(vmem_limit_bytes=1024 * 1024),
    )(*parts)


def store(a, b, out_a, out_b, sem):
    copies = [
        pltpu.make_async_copy(a, out_a, sem.at[0]),
        pltpu.make_async_copy(b, out_b, sem.at[1]),
    ]
    for c in copies:
        c.start()
    for c in copies:
        c.wait()


def solution(mesh):
    placed = (
        P("section", None, "tensor", None),
        P("section", None),
        P("section", "tensor", None, None),
        P("section", "tensor", None, None),
        P("section", "tensor", None, None),
        P("section", "tensor"),
        P("section", None, "tensor", None),
    )
    return jax.shard_map(
        functools.partial(on_device, mesh.shape["section"], mesh.shape["tensor"]),
        mesh=mesh,
        in_specs=placed,
        out_specs=(P("section", None, "tensor", None), P("section", None, "tensor", None)),
        check_vma=False,
    )
```

```python
import functools

import jax
import jax.numpy as jnp
from jax import lax
from jax.experimental import pallas as pl
from jax.experimental.pallas import tpu as pltpu
from jax.sharding import PartitionSpec as P

FB_DEV = 4
EPS = 1e-05
PAIR = 2
MESH = pl.DeviceIdType.MESH


def kernel(
    sections, tensors,
    tl_h, carry, gain, wg_h, wu_h, wd_h, dy_h,
    out, gback,
    xg, dyg, dyn, gn, gv, cown, wg, wu, wd, nb, db, xs, gu, dh, part, hb, dgu,
    stage, xr, zs, zr, wdt, wgt, tl, inv, last, lsem, ssem, rsem,
):
    line = tensors // PAIR
    mb, tokd, width = carry.shape[1:]
    per = mb * tokd
    half = line * per
    rows = PAIR * half
    blk = wg.shape[-1]
    slots = wg.shape[0]
    dblocks = width // blk
    s = lax.axis_index("section")
    t = lax.axis_index("tensor")
    z, x = t // PAIR, t % PAIR
    s_next, s_prev = (s + 1) % sections, (s + sections - 1) % sections

    def dev(sec, zt, other=False):
        return (sec, zt * PAIR + ((PAIR - 1 - x) if other else x))

    local = [
        pltpu.make_async_copy(tl_h, tl, lsem.at[6]),
        pltpu.make_async_copy(carry.at[0], cown, lsem.at[5]),
        pltpu.make_async_copy(dy_h.at[0], dyg.at[0, z], lsem.at[0]),
        pltpu.make_async_copy(gain, gv, lsem.at[4]),
        pltpu.make_async_copy(wg_h.at[0], wg, lsem.at[2]),
        pltpu.make_async_copy(wu_h.at[0], wu, lsem.at[3]),
        pltpu.make_async_copy(wd_h.at[0], wd, lsem.at[1]),
    ]
    for c in local:
        c.start()

    offsets = sorted((o for o in range(1 - line, line) if o), key=abs)

    def each(offs, body):
        for o in offs:
            zt = z + o

            @pl.when(jnp.logical_and(zt >= 0, zt < line))
            def _(zt=zt):
                body(zt)

    barrier = pltpu.get_barrier_semaphore()

    def greet(to):
        pl.semaphore_signal(barrier, inc=1, device_id=to, device_id_type=MESH)

    greet(dev(s, z, True))
    greet(dev(s_prev, z))
    greet(dev(s_prev, z, True))

    def greet_line(zt):
        greet(dev(s, zt))
        greet(dev(s_prev, zt))
    each(offsets, greet_line)
    pl.semaphore_wait(barrier, 2 * line + 1)

    def remote(src, dst, si, ri, to):
        return pltpu.make_async_remote_copy(
            src_ref=src, dst_ref=dst, send_sem=ssem.at[si], recv_sem=rsem.at[ri],
            device_id=to, device_id_type=MESH,
        )

    XZ, DYZ, FX, BX, FZ = (i * line for i in range(5))
    XX, DYX, BZ, DYB, GNB = (5 * line + i for i in range(5))
    SX, SDY, SW, SB, SG, SF = range(6)
    mate = dev(s, z, True)

    def x_line(zt):
        return remote(carry.at[0], xg.at[0, z], SX, XZ + z, dev(s_next, zt))

    def x_mate():
        return remote(carry.at[0], xg.at[1, z], SX, XX, dev(s_next, z, True))

    def x_relay(zt):
        return remote(xg.at[0, zt], xg.at[1, zt], SX, XX, mate)

    def dy_line(zt):
        return remote(dy_h.at[0], dyg.at[0, z], SDY, DYZ + z, dev(s, zt))

    def dy_mate():
        return remote(dy_h.at[0], dyg.at[1, z], SDY, DYX, mate)

    def dy_relay(zt):
        return remote(dyg.at[0, zt], dyg.at[1, zt], SDY, DYX, mate)

    def dy_back():
        return remote(dy_h.at[0], dyn, SDY, DYB, dev(s_prev, z))

    def gain_back():
        return remote(gain, gn, SG, GNB, dev(s_prev, z))

    def got(dst, ri):
        remote(dst, dst, 0, ri, mate).wait_recv()

    def gone(src, si):
        remote(src, src, si, 0, mate).wait_send()

    each(offsets, lambda zt: x_line(zt).start())
    x_line(z).start()
    x_mate().start()
    dy_mate().start()

    local[0].wait()
    p = jnp.int32(0)
    for f in range(FB_DEV):
        def cell(i, p, f=f):
            q = f * dblocks + i
            hit = tl[0, jnp.minimum(p, slots - 1)] == q
            inv[q] = jnp.where(hit, p, slots)
            return p + hit.astype(jnp.int32)
        p_new = lax.fori_loop(0, dblocks, cell, p, unroll=4)
        last[f] = jnp.where(p_new > p, p_new - 1, slots)
        p = p_new
    gu[slots] = jnp.zeros((rows, 2 * blk), jnp.float32)
    dh[slots] = jnp.zeros((rows, blk), jnp.float32)
    part[slots] = jnp.zeros((rows, blk), jnp.float32)

    def rows_of(ref, c, h):
        cols = pl.ds(pl.multiple_of(c * blk, blk), blk)
        pieces = []
        for d in range(line):
            for m in range(mb):
                pieces.append(ref[h, d, m, :, cols].astype(jnp.float32))
        return jnp.concatenate(pieces, axis=0)

    def f_of(k):
        return jnp.minimum(tl[0, k] // dblocks, FB_DEV - 1)

    def c_of(k):
        return tl[0, k] % dblocks

    def keep_of(k):
        return (f_of(k) == f_of(jnp.maximum(k - 1, 0))).astype(jnp.float32)

    def square(h):
        def body(c, acc):
            v = rows_of(xg, c, h)
            xs[c, h * half:(h + 1) * half] = v
            return acc + v * v
        return lax.fori_loop(0, dblocks, body, jnp.zeros((half, blk), jnp.float32), unroll=4)

    def norm(h):
        scale = lax.rsqrt(jnp.sum(square(h), axis=-1, keepdims=True) / width + EPS)

        @pl.loop(0, dblocks, unroll=4)
        def _(c):
            cols = pl.ds(pl.multiple_of(c * blk, blk), blk)
            mine = slice(h * half, (h + 1) * half)
            nb[c, mine] = (xs[c, mine] * scale * gv[:, cols]).astype(jnp.bfloat16)

    def pack_dy(h):
        @pl.loop(0, dblocks, unroll=4)
        def _(c):
            db[c, h * half:(h + 1) * half] = rows_of(dyg, c, h).astype(jnp.bfloat16)

    def turn(ref, src, at):
        @pl.loop(0, slots, unroll=8)
        def _(k):
            ref[k, at:at + blk] = src[k].T

    for i, (ref, src, at) in ((6, (wdt, wd, 0)), (4, (wgt, wg, 0)), (5, (wgt, wu, blk))):
        local[i].wait()
        turn(ref, src, at)
    each(offsets, lambda zt: dy_line(zt).start())
    def relay_x(zt):
        got(xg.at[0, zt], XZ + zt)
        x_relay(zt).start()
    each(offsets, relay_x)
    got(xg.at[0, z], XZ + z)
    dy_back().start()
    gain_back().start()
    local[3].wait()
    norm(0)
    def relay_dy(zt):
        got(dyg.at[0, zt], DYZ + zt)
        dy_relay(zt).start()
    each(offsets, relay_dy)
    for c in local[1:3]:
        c.wait()
    pack_dy(0)
    got(xg.at[1], XX)
    norm(1)

    def g_step(k, cur):
        w = jnp.concatenate([wg[k], wu[k]], axis=1)
        new = jnp.dot(nb[c_of(k)], w, preferred_element_type=jnp.float32)
        cur = cur * keep_of(k) + new
        gu[k] = cur
        return cur
    lax.fori_loop(0, slots, g_step, jnp.zeros((rows, 2 * blk), jnp.float32), unroll=slots)

    for f in range(FB_DEV):
        both = gu[last[f]]
        g, u = both[:, :blk], both[:, blk:]
        hb[f] = (g * jax.nn.sigmoid(g) * u).astype(jnp.bfloat16)

    def collect(a, h):
        @pl.loop(0, dblocks, unroll=4)
        def _(c):
            cols = pl.ds(pl.multiple_of(c * blk, blk), blk)
            mine = pl.ds(h * half, half)
            total = part[inv[c], mine]
            for f in range(1, FB_DEV):
                total = total + part[inv[f * dblocks + c], mine]
            for d in range(line):
                stage[a, h, d, :, cols] = total[d * per:(d + 1) * per].astype(jnp.bfloat16)

    def away(body):
        @pl.when(2 * z < line)
        def _():
            for zt in range(line):
                @pl.when(z != zt)
                def _(zt=zt):
                    body(zt)

        @pl.when(2 * z >= line)
        def _():
            for zt in range(line):
                @pl.when(z != zt)
                def _(zt=zt):
                    body(zt)

    def own(body):
        for zt in range(line):
            @pl.when(z == zt)
            def _(zt=zt):
                body(zt)

    def swap(a, base, zt):
        return remote(stage.at[a, 1, zt], xr.at[a, zt], SW, base + zt, mate)

    def f_out(zt):
        return remote(zs.at[0, zt], zr.at[0, z], SF + zt, FZ + z, dev(s, zt))

    def b_out(zt):
        return remote(zs.at[1, zt], zr.at[1, z], SB, BZ, dev(s_prev, zt))

    def o_step(k, _):
        part[k] = jnp.dot(hb[f_of(k)], wd[k], preferred_element_type=jnp.float32)
        return 0
    lax.fori_loop(0, slots, o_step, 0, unroll=slots)
    collect(0, 1)
    away(lambda zt: swap(0, FX, zt).start())
    collect(0, 0)

    got(dyg.at[1], DYX)
    pack_dy(1)

    def d_step(k, cur):
        new = jnp.dot(db[c_of(k)], wdt[k], preferred_element_type=jnp.float32)
        cur = cur * keep_of(k) + new
        dh[k] = cur
        return cur
    lax.fori_loop(0, slots, d_step, jnp.zeros((rows, blk), jnp.float32), unroll=slots)

    for f in range(FB_DEV):
        both = gu[last[f]]
        g, u = both[:, :blk], both[:, blk:]
        sg = jax.nn.sigmoid(g)
        dv = dh[last[f]]
        dgu[f, :, :blk] = (dv * u * sg * (1.0 + g * (1.0 - sg))).astype(jnp.bfloat16)
        dgu[f, :, blk:] = (dv * g * sg).astype(jnp.bfloat16)

    def b_step(k, _):
        part[k] = jnp.dot(dgu[f_of(k)], wgt[k], preferred_element_type=jnp.float32)
        return 0
    lax.fori_loop(0, slots, b_step, 0, unroll=slots)
    collect(1, 1)
    away(lambda zt: swap(1, BX, zt).start())
    swap(1, BX, z).start()
    swap(0, FX, z).start()
    collect(1, 0)

    def pair_sum(a, zt):
        return stage[a, 0, zt].astype(jnp.float32) + xr[a, zt].astype(jnp.float32)

    def f_send(zt):
        got(xr.at[0, zt], FX + zt)
        zs[0, zt] = pair_sum(0, zt).astype(jnp.bfloat16)
        f_out(zt).start()
    away(f_send)
    def b_send(zt):
        got(xr.at[1, zt], BX + zt)
        zs[1, zt] = pair_sum(1, zt).astype(jnp.bfloat16)
        b_out(zt).start()
    away(b_send)
    own(b_send)
    def f_keep(zt):
        got(xr.at[0, zt], FX + zt)
        zr[0, zt] = pair_sum(0, zt).astype(jnp.bfloat16)
    own(f_keep)
    each(offsets, lambda zt: got(zr.at[0, zt], FZ + zt))
    ffn = zr[0, 0].astype(jnp.float32)
    for d in range(1, line):
        ffn = ffn + zr[0, d].astype(jnp.float32)
    for m in range(mb):
        xo = xg[0, z, m].astype(jnp.float32)
        out[0, m] = (xo + ffn[m * tokd:(m + 1) * tokd]).astype(jnp.bfloat16)

    gone(xg, SX)
    gone(dyg, SDY)
    gone(gain, SG)
    gone(xr, SW)
    each(offsets, lambda zt: f_out(zt).wait_send())
    got(dyn, DYB)
    got(gn, GNB)
    scales, cubes = [], []
    for m in range(mb):
        xo = cown[m].astype(jnp.float32)
        sc = lax.rsqrt(jnp.mean(xo * xo, axis=-1, keepdims=True) + EPS)
        scales.append(sc)
        cubes.append(sc * sc * sc)
    got(zr.at[1], BZ)
    gnorm = zr[1, 0].astype(jnp.float32)
    for d in range(1, line):
        gnorm = gnorm + zr[1, d].astype(jnp.float32)
    for m in range(mb):
        xo = cown[m].astype(jnp.float32)
        gg = gn[...] * gnorm[m * tokd:(m + 1) * tokd]
        mixed = jnp.mean(xo * gg, axis=-1, keepdims=True)
        gx = dyn[m].astype(jnp.float32) + scales[m] * gg - xo * (cubes[m] * mixed)
        gback[0, m] = gx.astype(jnp.bfloat16)
    gone(zs.at[1], SB)


def on_device(sections, tensors, carry_in, norm_gain, w_gate, w_up, w_down, tile_list, grad_in):
    _, mb, tokd, width = carry_in.shape
    slots, blk = w_gate.shape[1], w_gate.shape[-1]
    line = tensors // PAIR
    per = mb * tokd
    half = line * per
    rows = PAIR * half
    dblocks = width // blk
    bf, f32 = jnp.bfloat16, jnp.float32
    V = pltpu.VMEM
    anyspec = pl.BlockSpec(memory_space=pl.ANY)
    parts = pl.pallas_call(
        functools.partial(kernel, sections, tensors),
        out_shape=[jax.ShapeDtypeStruct(carry_in.shape, bf)] * 2,
        in_specs=[pl.BlockSpec(memory_space=pltpu.HBM)] * 7,
        out_specs=[pl.BlockSpec(memory_space=pltpu.VMEM)] * 2,
        scratch_shapes=[
            V((PAIR, line, mb, tokd, width), bf),
            V((PAIR, line, mb, tokd, width), bf),
            V((mb, tokd, width), bf),
            V((1, width), f32),
            V((1, width), f32),
            V((mb, tokd, width), bf),
            V((slots, blk, blk), bf),
            V((slots, blk, blk), bf),
            V((slots, blk, blk), bf),
            V((dblocks, rows, blk), bf),
            V((dblocks, rows, blk), bf),
            V((dblocks, rows, blk), f32),
            V((slots + 1, rows, 2 * blk), f32),
            V((slots + 1, rows, blk), f32),
            V((slots + 1, rows, blk), f32),
            V((FB_DEV, rows, blk), bf),
            V((FB_DEV, rows, 2 * blk), bf),
            V((2, PAIR, line, per, width), bf),
            V((2, line, per, width), bf),
            V((2, line, per, width), bf),
            V((2, line, per, width), bf),
            V((slots, blk, blk), bf),
            V((slots, 2 * blk, blk), bf),
            pltpu.SMEM((1, slots), jnp.int32),
            pltpu.SMEM((FB_DEV * dblocks,), jnp.int32),
            pltpu.SMEM((FB_DEV,), jnp.int32),
            pltpu.SemaphoreType.DMA((7,)),
            pltpu.SemaphoreType.DMA((5 + line,)),
            pltpu.SemaphoreType.DMA((5 * line + 5,)),
        ],
        compiler_params=pltpu.CompilerParams(
            collective_id=0, has_side_effects=True, vmem_limit_bytes=48 * 1024 * 1024
        ),
    )(*(pltpu.with_memory_space_constraint(v, pltpu.HBM) for v in (tile_list, carry_in, norm_gain, w_gate, w_up, w_down, grad_in)))
    return pl.pallas_call(
        store,
        out_shape=[jax.ShapeDtypeStruct(carry_in.shape, bf)] * 2,
        in_specs=[pl.BlockSpec(memory_space=pltpu.VMEM)] * 2,
        out_specs=[anyspec] * 2,
        scratch_shapes=[pltpu.SemaphoreType.DMA((2,))],
        compiler_params=pltpu.CompilerParams(vmem_limit_bytes=1024 * 1024),
    )(*parts)


def store(a, b, out_a, out_b, sem):
    copies = [
        pltpu.make_async_copy(a, out_a, sem.at[0]),
        pltpu.make_async_copy(b, out_b, sem.at[1]),
    ]
    for c in copies:
        c.start()
    for c in copies:
        c.wait()


def solution(mesh):
    placed = (
        P("section", None, "tensor", None),
        P("section", None),
        P("section", "tensor", None, None),
        P("section", "tensor", None, None),
        P("section", "tensor", None, None),
        P("section", "tensor"),
        P("section", None, "tensor", None),
    )
    return jax.shard_map(
        functools.partial(on_device, mesh.shape["section"], mesh.shape["tensor"]),
        mesh=mesh,
        in_specs=placed,
        out_specs=(P("section", None, "tensor", None), P("section", None, "tensor", None)),
        check_vma=False,
    )
```
